32 devices in a mesh: view: 2 (over core), dom: 16 (over z, y, x).
Axes of the slice: x: 2, y: 2, z: 4, core: 2. Of those that a mesh axis runs over, the one named last changes fastest.
Arguments:
- features: bfloat16 [16384, 512], P('dom'), may hold values from -6 to 6
- feat_keep: int32 [2, 512], P('view'), may hold values 0 or 1
- w_first: bfloat16 [512, 512], replicated, may hold values from -0.25 to 0.25
- w_second: bfloat16 [512, 512], replicated, may hold values from -0.25 to 0.25
- adjacency: bfloat16 [2, 1024, 128, 128], P('view', 'dom'), may hold values from 0 to 0.015625
- tile_src: int32 [2, 128, 8], P('view', 'dom'), may hold values from 0 to 8, as said below
- halo_rows: int32 [16, 16, 8], P('dom'), may hold values from 0 to 1023
- halo_live: int32 [16, 16], P('dom'), may hold values from 0 to 8, as said below
- neg_pick: int32 [16, 16, 8], P('dom'), may hold values from 0 to 1023
Outputs:
- node_loss: float32 [2, 16384], P('view', 'dom')
- grad_first: float32 [512, 512], replicated
- grad_second: float32 [512, 512], replicated
The draws below stay inside these ranges and needn't reach their ends.
Inputs may be any that keep to these rules, and one draw needn't show every extreme that they name: `tile_src`: the last tile of the first block of every partition reads its last halo block. `halo_live`: some receiver gets 8 live rows from every sender.
All inputs are finite; a program needn't handle non-finite values. No bound on the sum of `feat_keep` on one device may be relied on, other than what follows from the above.
Results may differ from the reference program's by a relative error of at most 0.0015.
The reference program's roundings to bfloat16 on the way count: a program that leaves them out, or rounds other values in their place, can miss the bound.
Values may be sent and summed in bfloat16 or wider, within the bound.
No kernel may reach another device: no remote copies, remote signals or barrier semaphores. Data moves between devices by JAX's collectives and lax.ppermute only.
A program may use at most 128 MiB of HBM per device.

```python
import jax
import jax.numpy as jnp
from jax import lax

FEAT = 512
HID = 512
BS = 128
TPB = 8
CAP = 8
NEGR = 8
NBL = 8
NODES = 16384
N_DOM = 16


def draw_tile_src(key, part):
    block_total = NBL * N_DOM
    ext_blocks = NBL + N_DOM * CAP // BS
    base = jax.random.randint(jax.random.fold_in(key, 11), (2, block_total, TPB), 0, ext_blocks)
    first_block = jnp.arange(block_total) % NBL == 0
    forced = jnp.where(first_block, ext_blocks - 1, base[:, :, TPB - 1])
    return base.at[:, :, TPB - 1].set(forced).astype(jnp.int32)


def draw_halo_rows(key, part):
    base = jax.random.randint(jax.random.fold_in(key, 23), (N_DOM, N_DOM, CAP), 0, NBL * BS)
    target = jax.random.randint(jax.random.fold_in(key, 29), (N_DOM,), 0, N_DOM)
    return base.at[jnp.arange(N_DOM), target, 0].set(NBL * BS - 1).astype(jnp.int32)


def draw_halo_live(key, part):
    base = jax.random.randint(jax.random.fold_in(key, 37), (N_DOM, N_DOM), 0, CAP + 1)
    target = jax.random.randint(jax.random.fold_in(key, 41), (), 0, N_DOM)
    column = jnp.arange(N_DOM)[None, :] == target
    return jnp.where(column, CAP, base).astype(jnp.int32)


def draw_neg_pick(key, part):
    base = jax.random.randint(jax.random.fold_in(key, 53), (N_DOM, N_DOM, NEGR), 0, NBL * BS)
    target = jax.random.randint(jax.random.fold_in(key, 59), (N_DOM,), 0, N_DOM)
    return base.at[jnp.arange(N_DOM), target, 0].set(NBL * BS - 1).astype(jnp.int32)


def touch_ends(result, rng, low, high):
    longest = result.shape.index(max(result.shape))
    spots = []
    for shift in (0, 1):
        where = [jax.random.randint(jax.random.fold_in(rng, axis), (), 0, length) for axis, length in enumerate(result.shape)]
        where[longest] = (where[longest] + shift) % result.shape[longest]
        spots.append(tuple(where))
    return result.at[spots[0]].set(low).at[spots[1]].set(high)


def block_levels(stream_key, shape, split, smallest, high):
    def one(dim, shards_of):
        steps = jax.random.uniform(jax.random.fold_in(jax.random.fold_in(stream_key, 6), dim), (shards_of,), jnp.float32, smallest / len(split), high / len(split))
        return jnp.repeat(jnp.exp(steps), shape[dim] // shards_of).reshape((-1,) + (1,) * (len(shape) - dim - 1))

    gain = one(*split[0])
    for cut in split[1:]:
        gain = gain * one(*cut)
    return gain


def bell_draw(rng, dims, scale, bound, shards=(), kind=jnp.bfloat16):
    drawn = scale * jax.random.normal(rng, dims, jnp.float32)
    if shards:
        drawn = drawn * block_levels(rng, dims, shards, -0.22, 0.18)
    return jnp.clip(drawn, -bound, bound).astype(kind)


def setup_inputs(seed: int = 0) -> dict:
    seeds = jax.random.split(jax.random.key(seed), 10)
    features = bell_draw(seeds[0], (NODES, FEAT), 1.0, 6.0, ((0, 16),))
    feat_keep = touch_ends((jax.random.randint(seeds[1], (2, FEAT), 0, 4) < 3).astype(jnp.int32), jax.random.fold_in(seeds[1], 1), 0, 1)
    w_first = bell_draw(seeds[2], (FEAT, HID), FEAT ** -0.5, 0.25)
    w_second = bell_draw(seeds[3], (HID, HID), HID ** -0.5, 0.25)
    adjacency = jnp.clip(0.015625 * jax.random.uniform(seeds[4], (2, NODES // BS * TPB, BS, BS), jnp.float32) ** block_levels(seeds[4], (2, NODES // BS * TPB, BS, BS), ((0, 2), (1, 16)), -0.2, 0.2), 0.0, 0.015625).astype(jnp.bfloat16)
    tile_src = draw_tile_src(jax.random.fold_in(seeds[9], 71), 0)
    halo_rows = draw_halo_rows(jax.random.fold_in(seeds[9], 71), 0)
    halo_live = draw_halo_live(jax.random.fold_in(seeds[9], 71), 0)
    neg_pick = draw_neg_pick(jax.random.fold_in(seeds[9], 71), 0)
    return {"features": features, "feat_keep": feat_keep, "w_first": w_first, "w_second": w_second, "adjacency": adjacency, "tile_src": tile_src, "halo_rows": halo_rows, "halo_live": halo_live, "neg_pick": neg_pick}


inv_temp = 5.0
norm_eps = 1e-06

def mix_part(packed):
    ext_blocks, tiles, sources, inv_deg = packed
    picked = ext_blocks[sources].astype(jnp.float32)
    summed = jnp.einsum('ntij,ntjw->niw', tiles.astype(jnp.float32), picked)
    own_rows = ext_blocks[:sources.shape[0]].astype(jnp.float32)
    return ((own_rows + summed) * inv_deg[:, :, None]).astype(jnp.bfloat16)

def mix_back(packed):
    grad_mixed, tiles, sources, inv_deg = packed
    scaled = (grad_mixed * inv_deg[:, :, None]).astype(jnp.bfloat16)
    spread = jnp.einsum('ntij,niw->ntjw', tiles.astype(jnp.float32), scaled.astype(jnp.float32))
    total_blocks = NBL + N_DOM * CAP // BS
    ext_grad = jnp.zeros((total_blocks, BS, grad_mixed.shape[-1]), jnp.float32)
    ext_grad = ext_grad.at[sources].add(spread)
    return ext_grad.at[:NBL].add(scaled.astype(jnp.float32))

def contrast(packed):
    unit, partner, negatives = packed
    unit_f = unit.astype(jnp.float32)
    partner_f = partner.astype(jnp.float32)
    positive = inv_temp * lax.optimization_barrier(jnp.sum(unit_f * partner_f, axis=1))
    scores = inv_temp * jnp.dot(unit, negatives.T, preferred_element_type=jnp.float32)
    expo = jnp.exp(scores)
    total = jnp.exp(positive) + lax.optimization_barrier(jnp.sum(expo, axis=1))
    node_loss = jnp.log(total) - positive
    prob = (expo / total[:, None]).astype(jnp.bfloat16)
    own_share = jnp.exp(positive) / total
    g_anchor = inv_temp * ((own_share - 1.0)[:, None] * partner_f + jnp.dot(prob, negatives, preferred_element_type=jnp.float32))
    g_partner = inv_temp * (own_share - 1.0)[:, None] * unit_f
    g_neg = inv_temp * jnp.dot(prob.T, unit, preferred_element_type=jnp.float32)
    return (node_loss, g_anchor, g_partner, g_neg)

def reference(features, feat_keep, w_first, w_second, adjacency, tile_src, halo_rows, halo_live, neg_pick):
    part_rows = NBL * BS
    sender = jnp.arange(N_DOM, dtype=jnp.int32)[:, None, None]
    live_slots = jnp.arange(CAP, dtype=jnp.int32)[None, None, :] < halo_live[:, :, None]

    def halo_of(local):
        picked = local[sender, halo_rows] * live_slots[:, :, :, None].astype(local.dtype)
        return jnp.transpose(picked, (1, 0, 2, 3)).reshape(N_DOM, N_DOM * CAP, local.shape[-1])

    def halo_back(grad_ext, width):
        slots = grad_ext[:, NBL:].reshape(N_DOM, N_DOM, CAP, width)
        slots = jnp.transpose(slots, (1, 0, 2, 3)) * live_slots[:, :, :, None].astype(jnp.float32)
        own_part = grad_ext[:, :NBL].reshape(N_DOM, part_rows, width)
        return own_part.at[sender, halo_rows].add(slots)
    saved = []
    for view_index in range(2):
        tiles = adjacency[view_index].reshape(N_DOM, NBL, TPB, BS, BS)
        sources = tile_src[view_index].reshape(N_DOM, NBL, TPB)
        inv_deg = 1.0 / (1.0 + lax.optimization_barrier(jnp.sum(tiles.astype(jnp.float32), axis=(2, 4))))
        masked = features.reshape(N_DOM, part_rows, FEAT) * feat_keep[view_index].astype(jnp.bfloat16)
        ext_first = jnp.concatenate([masked, halo_of(masked)], 1).reshape(N_DOM, -1, BS, FEAT)
        mixed_first = lax.map(mix_part, (ext_first, tiles, sources, inv_deg)).reshape(NODES, FEAT)
        pre_act = jnp.dot(mixed_first, w_first, preferred_element_type=jnp.float32)
        hidden = jnp.maximum(pre_act, 0.0).astype(jnp.bfloat16).reshape(N_DOM, part_rows, HID)
        ext_second = jnp.concatenate([hidden, halo_of(hidden)], 1).reshape(N_DOM, -1, BS, HID)
        mixed_second = lax.map(mix_part, (ext_second, tiles, sources, inv_deg)).reshape(NODES, HID)
        projected = jnp.dot(mixed_second, w_second, preferred_element_type=jnp.float32)
        inv_norm = lax.rsqrt(lax.optimization_barrier(jnp.sum(projected * projected, axis=1, keepdims=True)) + norm_eps)
        normed = projected * inv_norm
        saved.append((tiles, sources, inv_deg, mixed_first, pre_act, mixed_second, inv_norm, normed, normed.astype(jnp.bfloat16)))
    losses = []
    anchors = []
    partners = []
    for view_index in range(2):
        unit = saved[view_index][8].reshape(N_DOM, part_rows, HID)
        other = saved[1 - view_index][8].reshape(N_DOM, part_rows, HID)
        picked = other[sender, neg_pick]
        negatives = jnp.transpose(picked, (1, 0, 2, 3)).reshape(N_DOM, N_DOM * NEGR, HID)
        node_loss, g_anchor, g_partner, g_neg = lax.map(contrast, (unit, other, negatives))
        g_neg = jnp.transpose(g_neg.reshape(N_DOM, N_DOM, NEGR, HID), (1, 0, 2, 3))
        g_partner = g_partner.at[sender, neg_pick].add(g_neg)
        losses.append(node_loss.reshape(NODES))
        anchors.append(g_anchor)
        partners.append(g_partner)
    grad_first = jnp.zeros((FEAT, HID), jnp.float32)
    grad_second = jnp.zeros((HID, HID), jnp.float32)
    for view_index in range(2):
        tiles, sources, inv_deg, mixed_first, pre_act, mixed_second, inv_norm, normed, unit = saved[view_index]
        g_emb = (anchors[view_index] + partners[1 - view_index]).reshape(NODES, HID)
        inner = lax.optimization_barrier(jnp.sum(normed * g_emb, axis=1, keepdims=True))
        g_proj = ((g_emb - normed * inner) * inv_norm).astype(jnp.bfloat16)
        grad_second = grad_second + jnp.dot(mixed_second.T, g_proj, preferred_element_type=jnp.float32)
        g_mixed = jnp.dot(g_proj, w_second.T, preferred_element_type=jnp.float32).reshape(N_DOM, NBL, BS, HID)
        grad_ext = lax.map(mix_back, (g_mixed, tiles, sources, inv_deg))
        g_hidden = halo_back(grad_ext, HID).reshape(NODES, HID)
        g_pre = jnp.where(pre_act > 0, g_hidden, 0.0).astype(jnp.bfloat16)
        grad_first = grad_first + jnp.dot(mixed_first.T, g_pre, preferred_element_type=jnp.float32)
    return (jnp.stack(losses), grad_first, grad_second)
```

```python
import jax
import jax.numpy as jnp
from jax import lax
from jax.sharding import PartitionSpec as P


inv_temp = 5.0
norm_eps = 1e-06


def swapped(array, axis, distance):
    return lax.ppermute(array, axis, [(i, i ^ 1 << distance) for i in range(lax.axis_size(axis))])


def exchange(array, axis, distance):
    return lax.ppermute(array, axis, [(i, i ^ distance) for i in range(lax.axis_size(axis))])


def index_stages():
    stages = [("view", lax.axis_size("view"), 1)]
    done = 1
    while done < lax.axis_size("dom"):
        ways = 4 if lax.axis_size("dom") // done % 4 == 0 else 2
        stages.append(("dom", ways, done))
        done *= ways
    return stages


def everyones_sum(pieces):
    stages = index_stages()
    for axis, ways, stride in stages:
        mine = lax.axis_index(axis) // stride % ways
        split = pieces.reshape((ways, pieces.shape[0] // ways) + pieces.shape[1:])
        arrived = [
            exchange(lax.dynamic_index_in_dim(split, mine ^ d, 0, False), axis, d * stride)
            for d in range(ways - 1, 0, -1)
        ]
        pieces = lax.dynamic_index_in_dim(split, mine, 0, False)
        for term in arrived:
            pieces = pieces + term
    for axis, ways, stride in stages[::-1]:
        mine = lax.axis_index(axis) // stride % ways
        held = [pieces] + [exchange(pieces, axis, d * stride) for d in range(1, ways)]
        ordered = []
        for j in range(ways):
            value = held[0]
            for d in range(1, ways):
                value = jnp.where(mine ^ j == d, held[d], value)
            ordered.append(value)
        pieces = jnp.concatenate(ordered, 0)
    return pieces


def mix_blocks(ext_blocks, tiles, sources, inv_deg):
    picked = ext_blocks[sources]
    summed = jnp.einsum("ntij,ntjw->niw", tiles, picked, preferred_element_type=jnp.float32)
    own_rows = ext_blocks[: sources.shape[0]].astype(jnp.float32)
    return ((own_rows + summed) * inv_deg[:, :, None]).astype(jnp.bfloat16)


def spread_back(grad_mixed, tiles, sources, inv_deg, total_blocks):
    scaled = (grad_mixed * inv_deg[:, :, None]).astype(jnp.bfloat16)
    spread = jnp.einsum("ntij,niw->ntjw", tiles, scaled, preferred_element_type=jnp.float32)
    ext_grad = jnp.zeros((total_blocks, grad_mixed.shape[1], grad_mixed.shape[2]), jnp.float32)
    ext_grad = ext_grad.at[sources].add(spread)
    return ext_grad.at[: sources.shape[0]].add(scaled.astype(jnp.float32))


def contrast(unit, partner, negatives):
    unit_f = unit.astype(jnp.float32)
    partner_f = partner.astype(jnp.float32)
    positive = inv_temp * jnp.sum(unit_f * partner_f, axis=1)
    scores = inv_temp * jnp.dot(unit, negatives.T, preferred_element_type=jnp.float32)
    expo = jnp.exp(scores)
    total = jnp.exp(positive) + jnp.sum(expo, axis=1)
    node_loss = jnp.log(total) - positive
    prob = (expo / total[:, None]).astype(jnp.bfloat16)
    own_share = jnp.exp(positive) / total
    share_less = own_share - 1.0
    g_anchor = inv_temp * (
        share_less[:, None] * partner_f
        + jnp.dot(prob, negatives, preferred_element_type=jnp.float32)
    )
    g_partner = inv_temp * share_less[:, None] * unit_f
    g_neg = inv_temp * jnp.dot(prob.T, unit, preferred_element_type=jnp.float32)
    return (node_loss, g_anchor, g_partner, g_neg, share_less)


def per_device(
    features, feat_keep, w_first, w_second, adjacency, tile_src, halo_rows, halo_live, neg_pick
):
    row_count, feat_width = features.shape
    hid_width = w_first.shape[1]
    block_rows = adjacency.shape[2]
    block_count = tile_src.shape[1]
    tile_count = tile_src.shape[2]
    part_count = lax.axis_size("dom")
    slot_cap = halo_rows.shape[2]
    neg_count = neg_pick.shape[2]
    tiles = adjacency[0].reshape(block_count, tile_count, block_rows, block_rows)
    sources = tile_src[0]
    inv_deg = 1.0 / (1.0 + jnp.sum(tiles.astype(jnp.float32), axis=(1, 3)))
    keep_cols = feat_keep[0].astype(jnp.bfloat16)
    send_rows = halo_rows[0]
    live_slots = lax.broadcasted_iota(jnp.int32, (part_count, slot_cap), 1) < halo_live[0][:, None]
    live_bf = live_slots.astype(jnp.bfloat16)[:, :, None]
    masked = features * keep_cols
    outgoing = masked[send_rows] * live_bf
    incoming = lax.all_to_all(outgoing, "dom", split_axis=0, concat_axis=0, tiled=True).reshape(
        part_count * slot_cap, feat_width
    )
    ext_first = jnp.concatenate([masked, incoming], 0).reshape(-1, block_rows, feat_width)
    mixed_first = mix_blocks(ext_first, tiles, sources, inv_deg).reshape(row_count, feat_width)
    pre_act = jnp.dot(mixed_first, w_first, preferred_element_type=jnp.float32)
    hidden = jnp.maximum(pre_act, 0.0).astype(jnp.bfloat16)
    hidden_out = hidden[send_rows] * live_bf
    hidden_in = lax.all_to_all(hidden_out, "dom", split_axis=0, concat_axis=0, tiled=True).reshape(
        part_count * slot_cap, hid_width
    )
    ext_second = jnp.concatenate([hidden, hidden_in], 0).reshape(-1, block_rows, hid_width)
    mixed_second = mix_blocks(ext_second, tiles, sources, inv_deg).reshape(row_count, hid_width)
    projected = jnp.dot(mixed_second, w_second, preferred_element_type=jnp.float32)
    inv_norm = lax.rsqrt(jnp.sum(projected * projected, axis=1, keepdims=True) + norm_eps)
    normed = projected * inv_norm
    unit = normed.astype(jnp.bfloat16)
    partner = swapped(unit, "view", 0)
    pick_rows = neg_pick[0].reshape(-1)
    neg_out = partner[neg_pick[0]]
    negatives = lax.all_to_all(neg_out, "dom", split_axis=0, concat_axis=0, tiled=True).reshape(
        part_count * neg_count, hid_width
    )
    node_loss, g_anchor, g_partner, g_neg, share_less = contrast(unit, partner, negatives)
    returned = lax.all_to_all(
        g_neg.reshape(part_count, neg_count, hid_width),
        "dom",
        split_axis=0,
        concat_axis=0,
        tiled=True,
    )
    g_partner = g_partner.at[pick_rows].add(returned.reshape(-1, hid_width))
    g_emb = g_anchor + swapped(g_partner, "view", 0)
    inner = jnp.sum(normed * g_emb, axis=1, keepdims=True)
    g_proj = ((g_emb - normed * inner) * inv_norm).astype(jnp.bfloat16)
    grad_second = jnp.einsum("ih,ik->hk", mixed_second, g_proj, preferred_element_type=jnp.float32)
    g_mixed = jnp.einsum("ik,hk->ih", g_proj, w_second, preferred_element_type=jnp.float32)
    ext_grad = spread_back(
        g_mixed.reshape(block_count, block_rows, hid_width),
        tiles,
        sources,
        inv_deg,
        ext_second.shape[0],
    )
    flat_grad = ext_grad.reshape(-1, hid_width)
    halo_grad = flat_grad[row_count:].reshape(part_count, slot_cap, hid_width)
    back_grad = lax.all_to_all(
        halo_grad.astype(jnp.bfloat16), "dom", split_axis=0, concat_axis=0, tiled=True
    ).astype(halo_grad.dtype)
    back_grad = back_grad * live_slots.astype(jnp.float32)[:, :, None]
    g_hidden = flat_grad[:row_count].at[send_rows.reshape(-1)].add(back_grad.reshape(-1, hid_width))
    g_pre = jnp.where(pre_act > 0, g_hidden, 0.0).astype(jnp.bfloat16)
    grad_first = jnp.einsum("if,ih->fh", mixed_first, g_pre, preferred_element_type=jnp.float32)
    pieces = jnp.concatenate([grad_first, grad_second], 0).reshape(2 * part_count, -1, hid_width)
    summed = everyones_sum(pieces).reshape(-1, hid_width)
    return (node_loss[None, :], summed[:feat_width], summed[feat_width:])


def solution(mesh):
    placed = (
        P("dom", None),
        P("view", None),
        P(),
        P(),
        P("view", "dom", None, None),
        P("view", "dom", None),
        P("dom", None, None),
        P("dom", None),
        P("dom", None, None),
    )
    return jax.shard_map(
        per_device,
        mesh=mesh,
        in_specs=placed,
        out_specs=(P("view", "dom"), P(), P()),
        check_vma=False,
    )
```

```python
import functools

import jax
import jax.numpy as jnp
from jax import lax
from jax.experimental import pallas as pl
from jax.experimental.pallas import tpu as pltpu
from jax.sharding import PartitionSpec as P


inv_temp = 5.0
norm_eps = 1e-06
BF = jnp.bfloat16
F32 = jnp.float32
LANES = 128


def exchange(array, axis, distance):
    return lax.ppermute(array, axis, [(i, i ^ distance) for i in range(lax.axis_size(axis))])


def index_stages():
    stages = [("view", lax.axis_size("view"), 1)]
    done = 1
    while done < lax.axis_size("dom"):
        ways = 4 if lax.axis_size("dom") // done % 4 == 0 else 2
        stages.append(("dom", ways, done))
        done *= ways
    return stages


def everyones_sum(pieces):
    stages = index_stages()
    for axis, ways, stride in stages:
        mine = lax.axis_index(axis) // stride % ways
        split = pieces.reshape((ways, pieces.shape[0] // ways) + pieces.shape[1:])
        arrived = [
            exchange(lax.dynamic_index_in_dim(split, mine ^ d, 0, False), axis, d * stride)
            for d in range(ways - 1, 0, -1)
        ]
        pieces = lax.dynamic_index_in_dim(split, mine, 0, False)
        for term in arrived:
            pieces = pieces + term
    for axis, ways, stride in stages[::-1]:
        mine = lax.axis_index(axis) // stride % ways
        held = [pieces] + [exchange(pieces, axis, d * stride) for d in range(1, ways)]
        ordered = []
        for j in range(ways):
            value = held[0]
            for d in range(1, ways):
                value = jnp.where(mine ^ j == d, held[d], value)
            ordered.append(value)
        pieces = jnp.concatenate(ordered, 0)
    return pieces


def to_others(rows):
    parts = lax.axis_size("dom")
    split = rows.reshape(parts, rows.shape[0] // parts, rows.shape[1])
    return lax.all_to_all(split, "dom", split_axis=0, concat_axis=0, tiled=True).reshape(rows.shape)


def kernel_call(body, outs, args, scratch=(), scalars=0, flops=0):
    moved = sum(a.size * a.dtype.itemsize for a in tuple(args) + tuple(outs))
    return pl.pallas_call(
        body,
        out_shape=tuple(jax.ShapeDtypeStruct(o.shape, o.dtype) for o in outs),
        in_specs=[pl.BlockSpec(memory_space=pltpu.SMEM)] * scalars
        + [pl.BlockSpec(memory_space=pltpu.VMEM)] * (len(args) - scalars),
        out_specs=tuple(pl.BlockSpec(memory_space=pltpu.VMEM) for _ in outs),
        scratch_shapes=list(scratch),
        cost_estimate=pl.CostEstimate(flops=flops, bytes_accessed=moved, transcendentals=0),
        name=body.__name__ if hasattr(body, "__name__") else body.func.__name__,
    )(*args)


def shape(rows, cols, dtype):
    return jax.ShapeDtypeStruct((rows, cols), dtype)


def dot(a, b, dims=((1,), (0,))):
    return lax.dot_general(a, b, (dims, ((), ())), preferred_element_type=F32)


def pick_matrix(slots, width):
    lanes = lax.broadcasted_iota(jnp.int32, (slots.shape[0], width), 1)
    return jnp.where(lanes == slots, 1.0, 0.0).astype(BF)


def put_matrix(slots, first, height):
    rows = lax.broadcasted_iota(jnp.int32, (height, slots.shape[1]), 0) + first
    return jnp.where(rows == slots, 1.0, 0.0).astype(BF)


def wide(column, width):
    return jnp.concatenate([column] * (width // LANES), axis=1)


def rows_at(index, size):
    return pl.ds(pl.multiple_of(index * size, size), size)


def mask_send(feat_ref, keep_ref, slots_ref, ext_ref, out_ref):
    rows = feat_ref.shape[0]
    masked = feat_ref[...] * keep_ref[...]
    ext_ref[:rows, :] = masked
    ext_ref[rows:, :] = jnp.zeros_like(ext_ref[rows:, :])
    out_ref[...] = dot(pick_matrix(slots_ref[...], rows), masked).astype(BF)


def own_sum(src_ref, tiles_ref, ext_ref, b):
    blocks, tpb = src_ref.shape
    bs = tiles_ref.shape[1]
    lhs = jnp.concatenate([tiles_ref[b * tpb + t] for t in range(tpb)], axis=1)
    rhs = jnp.concatenate(
        [ext_ref[rows_at(jnp.minimum(src_ref[b, t], blocks), bs), :] for t in range(tpb)], axis=0
    )
    return lhs, dot(lhs, rhs) + ext_ref[rows_at(b, bs), :].astype(F32)


def mix_own_first(src_ref, tiles_ref, ext_ref, acc_ref, inv_ref):
    blocks, tpb = src_ref.shape
    bs = tiles_ref.shape[1]

    @pl.loop(0, blocks)
    def _(b):
        lhs, total = own_sum(src_ref, tiles_ref, ext_ref, b)
        acc_ref[rows_at(b, bs), :] = total
        degree = dot(lhs, jnp.ones((tpb * bs, LANES), BF))
        inv_ref[rows_at(b, bs), :] = 1.0 / (1.0 + degree)


def mix_own_second(src_ref, tiles_ref, ext_ref, acc_ref):
    bs = tiles_ref.shape[1]

    @pl.loop(0, src_ref.shape[0])
    def _(b):
        acc_ref[rows_at(b, bs), :] = own_sum(src_ref, tiles_ref, ext_ref, b)[1]


def mix_halo(src_ref, tiles_ref, acc_ref, inv_ref, halo_ref, mixed_ref, total):
    blocks, tpb = src_ref.shape
    bs = tiles_ref.shape[1]
    width = mixed_ref.shape[1]

    @pl.loop(0, blocks)
    def _(b):
        here = rows_at(b, bs)
        total[...] = acc_ref[here, :]
        for t in range(tpb):
            source = src_ref[b, t] - blocks

            @pl.when(source >= 0)
            def _():
                total[...] += dot(tiles_ref[b * tpb + t], halo_ref[rows_at(source, bs), :])

        mixed_ref[here, :] = (total[...] * wide(inv_ref[here, :], width)).astype(BF)


def first_layer(
    src_ref, tiles_ref, acc_ref, inv_ref, halo_ref, w_ref, slots_ref,
    mixed_ref, alive_ref, ext_ref, out_ref, total
):
    rows = mixed_ref.shape[0]
    mix_halo(src_ref, tiles_ref, acc_ref, inv_ref, halo_ref, mixed_ref, total)
    step = rows // 4

    @pl.loop(0, 4)
    def _(c):
        here = rows_at(c, step)
        pre = dot(mixed_ref[here, :], w_ref[...])
        alive_ref[here, :] = jnp.where(pre > 0, 1.0, 0.0).astype(BF)
        ext_ref[here, :] = jnp.maximum(pre, 0.0).astype(BF)

    ext_ref[rows:, :] = jnp.zeros_like(ext_ref[rows:, :])
    out_ref[...] = dot(pick_matrix(slots_ref[...], rows), ext_ref[:rows, :]).astype(BF)


def second_layer(
    src_ref, tiles_ref, acc_ref, inv_ref, halo_ref, w_ref, slots_ref,
    mixed_ref, normed_ref, scale_ref, unit_ref, out_ref, total
):
    rows = mixed_ref.shape[0]
    mix_halo(src_ref, tiles_ref, acc_ref, inv_ref, halo_ref, mixed_ref, total)
    step = rows // 4

    @pl.loop(0, 4)
    def _(c):
        here = rows_at(c, step)
        projected = dot(mixed_ref[here, :], w_ref[...])
        scale = lax.rsqrt(jnp.sum(projected * projected, axis=1, keepdims=True) + norm_eps)
        normed = projected * scale
        normed_ref[here, :] = normed
        scale_ref[here, :] = jnp.broadcast_to(scale, (step, LANES))
        unit_ref[here, :] = normed.astype(BF)

    out_ref[...] = dot(pick_matrix(slots_ref[...], rows), unit_ref[...]).astype(BF)


def soft_terms(anchor, negatives, positive):
    expo = jnp.exp(inv_temp * dot(anchor, negatives, ((1,), (1,))))
    top = jnp.exp(positive)
    total = top + jnp.sum(expo, axis=1, keepdims=True)
    return (expo / total).astype(BF), top / total - 1.0, total


def contrast_other(unit_ref, other_ref, neg_ref, share_ref, positive_ref, grad_ref):
    rows = unit_ref.shape[0]
    step = rows // 4
    grad_ref[...] = jnp.zeros_like(grad_ref)

    @pl.loop(0, 4)
    def _(c):
        here = rows_at(c, step)
        other = other_ref[here, :]
        product = unit_ref[here, :].astype(F32) * other.astype(F32)
        positive = inv_temp * jnp.sum(product, axis=1, keepdims=True)
        prob, share, _ = soft_terms(other, neg_ref[...], positive)
        share_ref[here, :] = jnp.broadcast_to(share, (step, LANES))
        positive_ref[here, :] = jnp.broadcast_to(positive, (step, LANES))
        grad_ref[...] += inv_temp * dot(prob, other, ((0,), (0,)))


def contrast_own(unit_ref, other_ref, neg_ref, share_ref, positive_ref, loss_ref, grad_ref):
    rows, width = unit_ref.shape
    step = rows // 4

    @pl.loop(0, 4)
    def _(c):
        here = rows_at(c, step)
        positive = positive_ref[here, :][:, :1]
        prob, share, total = soft_terms(unit_ref[here, :], neg_ref[...], positive)
        loss_ref[here, :] = jnp.broadcast_to(jnp.log(total) - positive, (step, LANES))
        other = other_ref[here, :].astype(F32)
        anchor = share * other + dot(prob, neg_ref[...])
        partner = wide(share_ref[here, :], width) * other
        grad_ref[here, :] = inv_temp * anchor + inv_temp * partner


def back_project(
    src_ref, tiles_ref, part_ref, back_ref, slots_ref, normed_ref, scale_ref, w_ref, inv_ref,
    proj_ref, scaled_ref, out_ref, terms, halo
):
    blocks, tpb = src_ref.shape
    bs = tiles_ref.shape[1]
    rows, width = part_ref.shape
    count = back_ref.shape[0]
    left = back_ref[...]
    for k in range(3):
        term = left.astype(BF)
        terms[k * count : (k + 1) * count, :] = term
        left = left - term.astype(F32)
    step = rows // 4

    @pl.loop(0, 4)
    def _(c):
        here = rows_at(c, step)
        put = put_matrix(slots_ref[...], c * step, step)
        grad = part_ref[here, :] + dot(jnp.concatenate([put] * 3, axis=1), terms[...])
        normed = normed_ref[here, :]
        inner = jnp.sum(normed * grad, axis=1, keepdims=True)
        proj = ((grad - normed * inner) * wide(scale_ref[here, :], width)).astype(BF)
        proj_ref[here, :] = proj
        mixed = dot(proj, w_ref[...], ((1,), (1,)))
        scaled_ref[here, :] = (mixed * wide(inv_ref[here, :], width)).astype(BF)

    halo[...] = jnp.zeros_like(halo)

    @pl.loop(0, blocks)
    def _(b):
        for t in range(tpb):
            source = src_ref[b, t] - blocks

            @pl.when(source >= 0)
            def _():
                halo[rows_at(source, bs), :] += dot(
                    tiles_ref[b * tpb + t], scaled_ref[rows_at(b, bs), :], ((0,), (0,))
                )

    out_ref[...] = halo[...].astype(BF)


def back_own(src_ref, tiles_ref, scaled_ref, own_ref, total):
    blocks, tpb = src_ref.shape
    bs = tiles_ref.shape[1]
    rows = scaled_ref.shape[0]
    total[:rows, :] = scaled_ref[...].astype(F32)

    @pl.loop(0, blocks)
    def _(b):
        grad = scaled_ref[rows_at(b, bs), :]
        for t in range(tpb):
            there = rows_at(jnp.minimum(src_ref[b, t], blocks), bs)
            total[there, :] += dot(tiles_ref[b * tpb + t], grad, ((0,), (0,)))

    own_ref[...] = total[:rows, :]


def weight_grad(mixed_ref, grad_ref, out_ref):
    out_ref[...] = dot(mixed_ref[...], grad_ref[...], ((0,), (0,)))


def back_first(own_ref, back_ref, slots_ref, alive_ref, mixed_ref, out_ref, grads):
    rows = own_ref.shape[0]
    step = rows // 4

    @pl.loop(0, 4)
    def _(c):
        here = rows_at(c, step)
        put = put_matrix(slots_ref[...], c * step, step)
        grad = own_ref[here, :] + dot(put, back_ref[...])
        grads[here, :] = jnp.where(alive_ref[here, :].astype(F32) > 0, grad, 0.0).astype(BF)

    out_ref[...] = dot(mixed_ref[...], grads[...], ((0,), (0,)))


def per_device(
    features, feat_keep, w_first, w_second, adjacency, tile_src, halo_rows, halo_live, neg_pick
):
    rows, feat = features.shape
    hid = w_first.shape[1]
    bs = adjacency.shape[2]
    blocks, tpb = tile_src.shape[1:]
    parts = lax.axis_size("dom")
    cap = halo_rows.shape[2]
    slots = parts * cap
    picks = parts * neg_pick.shape[2]
    tiles = adjacency[0]
    src = tile_src[0]
    keep = feat_keep.astype(BF)
    live = lax.broadcasted_iota(jnp.int32, (parts, cap), 1) < halo_live[0][:, None]
    sent = jnp.where(live, halo_rows[0], -1)
    sent_col, sent_row = sent.reshape(slots, 1), sent.reshape(1, slots)
    pick_col, pick_row = neg_pick[0].reshape(picks, 1), neg_pick[0].reshape(1, picks)
    mix_flops = 2 * blocks * tpb * bs * bs * hid
    dense_flops = 2 * rows * feat * hid

    ext, outgoing = kernel_call(
        mask_send, [shape(rows + bs, feat, BF), shape(slots, feat, BF)], [features, keep, sent_col]
    )
    incoming = to_others(outgoing)
    acc, inv_deg = kernel_call(
        mix_own_first, [shape(rows, feat, F32), shape(rows, LANES, F32)], [src, tiles, ext],
        scalars=1, flops=mix_flops,
    )
    mixed_first, alive, ext, outgoing = kernel_call(
        first_layer,
        [shape(rows, feat, BF), shape(rows, hid, BF), shape(rows + bs, hid, BF), shape(slots, hid, BF)],
        [src, tiles, acc, inv_deg, incoming, w_first, sent_col],
        [pltpu.VMEM((bs, feat), F32)], scalars=1, flops=dense_flops,
    )
    incoming = to_others(outgoing)
    (acc,) = kernel_call(
        mix_own_second, [shape(rows, hid, F32)], [src, tiles, ext], scalars=1, flops=mix_flops
    )
    mixed_second, normed, scale, unit, outgoing = kernel_call(
        second_layer,
        [shape(rows, hid, BF), shape(rows, hid, F32), shape(rows, LANES, F32), shape(rows, hid, BF),
         shape(picks, hid, BF)],
        [src, tiles, acc, inv_deg, incoming, w_second, pick_col],
        [pltpu.VMEM((bs, hid), F32)], scalars=1, flops=dense_flops,
    )
    other = exchange(unit, "view", 1)
    neg_other = to_others(outgoing)
    neg_own = exchange(neg_other, "view", 1)
    share, positive, grad_neg = kernel_call(
        contrast_other,
        [shape(rows, LANES, F32), shape(rows, LANES, F32), shape(picks, hid, F32)],
        [unit, other, neg_other],
    )
    returned = to_others(grad_neg)
    loss, part = kernel_call(
        contrast_own, [shape(rows, LANES, F32), shape(rows, hid, F32)],
        [unit, other, neg_own, share, positive],
    )
    proj, scaled, outgoing = kernel_call(
        back_project,
        [shape(rows, hid, BF), shape(rows, hid, BF), shape(slots, hid, BF)],
        [src, tiles, part, returned, pick_row, normed, scale, w_second, inv_deg],
        [pltpu.VMEM((3 * picks, hid), BF), pltpu.VMEM((slots, hid), F32)],
        scalars=1, flops=dense_flops,
    )
    returned = to_others(outgoing)
    (own,) = kernel_call(
        back_own, [shape(rows, hid, F32)], [src, tiles, scaled],
        [pltpu.VMEM((rows + bs, hid), F32)], scalars=1, flops=mix_flops,
    )
    (grad_second,) = kernel_call(
        weight_grad, [shape(hid, hid, F32)], [mixed_second, proj], flops=dense_flops
    )
    (grad_first,) = kernel_call(
        back_first, [shape(feat, hid, F32)], [own, returned, sent_row, alive, mixed_first],
        [pltpu.VMEM((rows, hid), BF)], flops=dense_flops,
    )
    pieces = jnp.concatenate([grad_first, grad_second], 0).reshape(2 * parts, -1, hid)
    summed = everyones_sum(pieces).reshape(-1, hid)
    return (loss[:, 0][None, :], summed[:feat], summed[feat:])


def solution(mesh):
    placed = (
        P("dom", None),
        P("view", None),
        P(),
        P(),
        P("view", "dom", None, None),
        P("view", "dom", None),
        P("dom", None, None),
        P("dom", None),
        P("dom", None, None),
    )
    return jax.shard_map(
        per_device,
        mesh=mesh,
        in_specs=placed,
        out_specs=(P("view", "dom"), P(), P()),
        check_vma=False,
    )
```

```python
import math

import jax
import jax.numpy as jnp
from jax import lax
from jax.experimental import pallas as pl
from jax.experimental.pallas import tpu as pltpu
from jax.sharding import PartitionSpec as P


inv_temp = 5.0
norm_eps = 1e-06
BF = jnp.bfloat16
F32 = jnp.float32
LANES = 128
SLACK = 6 * 2**20


def exchange(array, axis, distance):
    return lax.ppermute(array, axis, [(i, i ^ distance) for i in range(lax.axis_size(axis))])


def index_stages():
    stages = []
    done = 1
    while done < lax.axis_size("dom"):
        ways = 4 if lax.axis_size("dom") // done % 4 == 0 else 2
        stages.append(("dom", ways, done))
        done *= ways
    return stages


def everyones_sum(pieces):
    stages = index_stages()
    for axis, ways, stride in stages:
        mine = lax.axis_index(axis) // stride % ways
        split = pieces.reshape((ways, pieces.shape[0] // ways) + pieces.shape[1:])
        arrived = [
            exchange(lax.dynamic_index_in_dim(split, mine ^ d, 0, False), axis, d * stride)
            for d in range(ways - 1, 0, -1)
        ]
        pieces = lax.dynamic_index_in_dim(split, mine, 0, False)
        for term in arrived:
            pieces = pieces + term
    for axis, ways, stride in stages[::-1]:
        mine = lax.axis_index(axis) // stride % ways
        held = [pieces] + [exchange(pieces, axis, d * stride) for d in range(1, ways)]
        ordered = []
        for j in range(ways):
            value = held[0]
            for d in range(1, ways):
                value = jnp.where(mine ^ j == d, held[d], value)
            ordered.append(value)
        pieces = jnp.concatenate(ordered, 0)
    return pieces


def to_others(rows, *live):
    parts = lax.axis_size("dom")
    rows, live = lax.optimization_barrier((rows, live))
    split = rows.reshape(parts, rows.shape[0] // parts, rows.shape[1])
    moved = lax.all_to_all(split, "dom", split_axis=0, concat_axis=0, tiled=True)
    moved, live = lax.optimization_barrier((moved, live))
    return moved.reshape(rows.shape), *live


def kernel_call(body, outs, args, scratch=(), scalars=0, flops=0):
    moved = sum(a.size * a.dtype.itemsize for a in tuple(args) + tuple(outs))
    held = sum(math.prod(a.shape) * a.dtype.itemsize for a in scratch)
    return pl.pallas_call(
        body,
        out_shape=tuple(jax.ShapeDtypeStruct(o.shape, o.dtype) for o in outs),
        in_specs=[pl.BlockSpec(memory_space=pltpu.SMEM)] * scalars
        + [pl.BlockSpec(memory_space=pltpu.VMEM)] * (len(args) - scalars),
        out_specs=tuple(pl.BlockSpec(memory_space=pltpu.VMEM) for _ in outs),
        scratch_shapes=list(scratch),
        cost_estimate=pl.CostEstimate(flops=flops, bytes_accessed=moved, transcendentals=0),
        compiler_params=pltpu.CompilerParams(vmem_limit_bytes=moved + held + SLACK),
        name=body.__name__ if hasattr(body, "__name__") else body.func.__name__,
    )(*args)


def shape(rows, cols, dtype):
    return jax.ShapeDtypeStruct((rows, cols), dtype)


def dot(a, b, dims=((1,), (0,))):
    return lax.dot_general(a, b, (dims, ((), ())), preferred_element_type=F32)


def pick_matrix(slots_ref, live_ref, place, width):
    cap, parts = slots_ref.shape

    @pl.loop(0, parts)
    def _(r):
        rows = lax.broadcasted_iota(jnp.int32, (cap, LANES), 0)
        slots = jnp.full((cap, LANES), -1, jnp.int32)
        for c in range(cap):
            slot = slots_ref[c, r]
            if live_ref is not None:
                slot = jnp.where(c < live_ref[0, r], slot, -1)
            slots = jnp.where(rows == c, slot, slots)
        place[rows_at(r, cap), :] = slots

    slots = place[...]
    lanes = lax.broadcasted_iota(jnp.int32, slots.shape, 1)
    columns = [
        jnp.where(slots == lanes + first, 1.0, 0.0).astype(BF) for first in range(0, width, LANES)
    ]
    return jnp.concatenate(columns, axis=1)


def wide(column, width):
    return jnp.concatenate([column] * (width // LANES), axis=1)


def rows_at(index, size):
    return pl.ds(pl.multiple_of(index * size, size), size)


def mask_send(slots_ref, live_ref, feat_ref, keep_ref, out_ref, pick_ref, place):
    pick_ref[...] = pick_matrix(slots_ref, live_ref, place, feat_ref.shape[0])
    picked = dot(pick_ref[...], feat_ref[...])
    out_ref[...] = picked.astype(BF) * keep_ref[...].astype(F32).astype(BF)


def tile_row(tiles_ref, b, tpb):
    return jnp.concatenate([tiles_ref[b * tpb + t] for t in range(tpb)], axis=1)


def mixed_sum(src_ref, tiles, ext, b, bs):
    picked = [ext[rows_at(src_ref[b, t], bs), :] for t in range(src_ref.shape[1])]
    return dot(tiles, jnp.concatenate(picked, axis=0)) + ext[rows_at(b, bs), :].astype(F32)


def first_layer(
    src_ref, picks_ref, feat_ref, keep_ref, halo_ref, tiles_ref, w_ref, send_ref,
    mixed_ref, alive_ref, hidden_ref, inv_ref, out_ref, pick_ref, ext, place
):
    blocks, tpb = src_ref.shape
    bs = tiles_ref.shape[1]
    rows, width = feat_ref.shape
    ext[:rows, :] = feat_ref[...] * keep_ref[...].astype(F32).astype(BF)
    ext[rows:, :] = halo_ref[...]

    @pl.loop(0, blocks)
    def _(b):
        here = rows_at(b, bs)
        tiles = tile_row(tiles_ref, b, tpb)
        inv = 1.0 / (1.0 + dot(tiles, jnp.ones((tpb * bs, LANES), BF)))
        inv_ref[here, :] = inv
        mixed_ref[here, :] = (mixed_sum(src_ref, tiles, ext, b, bs) * wide(inv, width)).astype(BF)

    step = rows // 4

    @pl.loop(0, 4)
    def _(c):
        here = rows_at(c, step)
        pre = dot(mixed_ref[here, :], w_ref[...])
        alive_ref[here, :] = jnp.where(pre > 0, 1.0, 0.0).astype(BF)
        hidden_ref[here, :] = jnp.maximum(pre, 0.0).astype(BF)

    out_ref[...] = dot(send_ref[...], hidden_ref[...]).astype(BF)
    pick_ref[...] = pick_matrix(picks_ref, None, place, rows)


def second_layer(
    src_ref, hidden_ref, halo_ref, tiles_ref, inv_ref, w_ref, pick_ref,
    mixed_ref, normed_ref, scale_ref, unit_ref, out_ref, ext
):
    blocks, tpb = src_ref.shape
    bs = tiles_ref.shape[1]
    rows, width = hidden_ref.shape
    ext[:rows, :] = hidden_ref[...]
    ext[rows:, :] = halo_ref[...]

    @pl.loop(0, blocks)
    def _(b):
        here = rows_at(b, bs)
        total = mixed_sum(src_ref, tile_row(tiles_ref, b, tpb), ext, b, bs)
        mixed_ref[here, :] = (total * wide(inv_ref[here, :], width)).astype(BF)

    step = rows // 4

    @pl.loop(0, 4)
    def _(c):
        here = rows_at(c, step)
        projected = dot(mixed_ref[here, :], w_ref[...])
        scale = lax.rsqrt(jnp.sum(projected * projected, axis=1, keepdims=True) + norm_eps)
        normed = projected * scale
        normed_ref[here, :] = normed
        scale_ref[here, :] = jnp.broadcast_to(scale, (step, LANES))
        unit_ref[here, :] = normed.astype(BF)

    out_ref[...] = dot(pick_ref[...], unit_ref[...]).astype(BF)


def soft_terms(anchor, negatives, positive):
    expo = jnp.exp(inv_temp * dot(anchor, negatives, ((1,), (1,))))
    top = jnp.exp(positive)
    total = top + jnp.sum(expo, axis=1, keepdims=True)
    return (expo / total).astype(BF), top / total - 1.0, total


def contrast_other(unit_ref, other_ref, neg_ref, share_ref, positive_ref, grad_ref):
    rows = unit_ref.shape[0]
    step = rows // 4
    grad_ref[...] = jnp.zeros_like(grad_ref)

    @pl.loop(0, 4)
    def _(c):
        here = rows_at(c, step)
        other = other_ref[here, :]
        product = unit_ref[here, :].astype(F32) * other.astype(F32)
        positive = inv_temp * jnp.sum(product, axis=1, keepdims=True)
        prob, share, _ = soft_terms(other, neg_ref[...], positive)
        share_ref[here, :] = jnp.broadcast_to(share, (step, LANES))
        positive_ref[here, :] = jnp.broadcast_to(positive, (step, LANES))
        grad_ref[...] += inv_temp * dot(prob, other, ((0,), (0,)))


def backward(
    src_ref, tiles_ref, unit_ref, other_ref, neg_ref, share_ref, positive_ref, back_ref, pick_ref,
    normed_ref, scale_ref, w_ref, inv_ref, mixed_ref,
    loss_ref, own_ref, out_ref, grad_ref, terms, proj_ref, scaled_ref, total
):
    blocks, tpb = src_ref.shape
    bs = tiles_ref.shape[1]
    rows, width = unit_ref.shape
    count = back_ref.shape[0]
    left = back_ref[...]
    for k in range(3):
        term = left.astype(BF)
        terms[k * count : (k + 1) * count, :] = term
        left = left - term.astype(F32)
    step = rows // 4

    @pl.loop(0, 4)
    def _(c):
        here = rows_at(c, step)
        positive = positive_ref[here, :][:, :1]
        prob, share, whole = soft_terms(unit_ref[here, :], neg_ref[...], positive)
        loss_ref[here, :] = jnp.broadcast_to(jnp.log(whole) - positive, (step, LANES))
        other = other_ref[here, :].astype(F32)
        anchor = share * other + dot(prob, neg_ref[...])
        partner = wide(share_ref[here, :], width) * other
        put = pick_ref[:, here]
        came = dot(jnp.concatenate([put] * 3, axis=0), terms[...], ((0,), (0,)))
        grad = inv_temp * anchor + (inv_temp * partner + came)
        normed = normed_ref[here, :]
        inner = jnp.sum(normed * grad, axis=1, keepdims=True)
        proj = ((grad - normed * inner) * wide(scale_ref[here, :], width)).astype(BF)
        proj_ref[here, :] = proj
        mixed = dot(proj, w_ref[...], ((1,), (1,)))
        scaled = (mixed * wide(inv_ref[here, :], width)).astype(BF)
        scaled_ref[here, :] = scaled
        total[here, :] = scaled.astype(F32)

    total[rows:, :] = jnp.zeros_like(total[rows:, :])

    @pl.loop(0, blocks)
    def _(b):
        grad = scaled_ref[rows_at(b, bs), :]
        for t in range(tpb):
            there = rows_at(src_ref[b, t], bs)
            total[there, :] += dot(tiles_ref[b * tpb + t], grad, ((0,), (0,)))

    own_ref[...] = total[:rows, :]
    out_ref[...] = total[rows:, :].astype(BF)
    grad_ref[...] = dot(mixed_ref[...], proj_ref[...], ((0,), (0,)))


def finish(view_ref, own_ref, back_ref, send_ref, alive_ref, mixed_ref, second_ref, keep_ref, give_ref, grads):
    rows = own_ref.shape[0]
    step = rows // 4

    @pl.loop(0, 4)
    def _(c):
        here = rows_at(c, step)
        grad = own_ref[here, :] + dot(send_ref[:, here], back_ref[...], ((0,), (0,)))
        grads[here, :] = jnp.where(alive_ref[here, :].astype(F32) > 0, grad, 0.0).astype(BF)

    first = dot(mixed_ref[...], grads[...], ((0,), (0,)))
    view = view_ref[0]

    @pl.when(view == 0)
    def _():
        keep_ref[...] = first
        give_ref[...] = second_ref[...]

    @pl.when(view != 0)
    def _():
        keep_ref[...] = second_ref[...]
        give_ref[...] = first


def per_device(
    features, feat_keep, w_first, w_second, adjacency, tile_src, halo_rows, halo_live, neg_pick
):
    rows, feat = features.shape
    hid = w_first.shape[1]
    bs = adjacency.shape[2]
    blocks, tpb = tile_src.shape[1:]
    parts = lax.axis_size("dom")
    slots = parts * halo_rows.shape[2]
    picks = parts * neg_pick.shape[2]
    tiles = adjacency[0]
    src = tile_src[0]
    mix_flops = 2 * blocks * tpb * bs * bs * hid
    dense_flops = 2 * rows * feat * hid

    halo_slots = jnp.swapaxes(halo_rows, 1, 2)[0]
    neg_slots = jnp.swapaxes(neg_pick, 1, 2)[0]
    view = lax.axis_index("view").reshape(1)
    outgoing, send = kernel_call(
        mask_send, [shape(slots, feat, BF), shape(slots, rows, BF)],
        [halo_slots, halo_live, features, feat_keep],
        [pltpu.VMEM((slots, LANES), jnp.int32)], scalars=2,
    )
    incoming, send, src, neg_slots, view = to_others(outgoing, send, src, neg_slots, view)
    mixed_first, alive, hidden, inv_deg, outgoing, pick = kernel_call(
        first_layer,
        [shape(rows, feat, BF), shape(rows, hid, BF), shape(rows, hid, BF), shape(rows, LANES, F32),
         shape(slots, hid, BF), shape(picks, rows, BF)],
        [src, neg_slots, features, feat_keep, incoming, tiles, w_first, send],
        [pltpu.VMEM((rows + slots, feat), BF), pltpu.VMEM((picks, LANES), jnp.int32)],
        scalars=2, flops=mix_flops + dense_flops,
    )
    incoming, hidden, inv_deg, pick = to_others(outgoing, hidden, inv_deg, pick)
    mixed_second, normed, scale, unit, outgoing = kernel_call(
        second_layer,
        [shape(rows, hid, BF), shape(rows, hid, F32), shape(rows, LANES, F32), shape(rows, hid, BF),
         shape(picks, hid, BF)],
        [src, hidden, incoming, tiles, inv_deg, w_second, pick],
        [pltpu.VMEM((rows + slots, hid), BF)], scalars=1, flops=mix_flops + dense_flops,
    )
    other = exchange(unit, "view", 1)
    neg_other, unit = to_others(outgoing, unit)
    neg_own = exchange(neg_other, "view", 1)
    share, positive, grad_neg = kernel_call(
        contrast_other,
        [shape(rows, LANES, F32), shape(rows, LANES, F32), shape(picks, hid, F32)],
        [unit, other, neg_other],
    )
    returned, neg_own, share, positive, unit, other = to_others(
        grad_neg, neg_own, share, positive, unit, other
    )
    loss, own, outgoing, grad_second = kernel_call(
        backward,
        [shape(rows, LANES, F32), shape(rows, hid, F32), shape(slots, hid, BF), shape(hid, hid, F32)],
        [src, tiles, unit, other, neg_own, share, positive, returned, pick, normed, scale,
         w_second, inv_deg, mixed_second],
        [pltpu.VMEM((3 * picks, hid), BF), pltpu.VMEM((rows, hid), BF), pltpu.VMEM((rows, hid), BF),
         pltpu.VMEM((rows + slots, hid), F32)],
        scalars=1, flops=mix_flops + 2 * dense_flops,
    )
    loss = loss[:, 0][None, :]
    returned, own, grad_second, view, loss = to_others(outgoing, own, grad_second, view, loss)
    kept, given = kernel_call(
        finish, [shape(hid, hid, F32), shape(hid, hid, F32)],
        [view, own, returned, send, alive, mixed_first, grad_second],
        [pltpu.VMEM((rows, hid), BF)], scalars=1, flops=dense_flops,
    )
    pieces = (kept + exchange(given, "view", 1)).reshape(parts, -1, hid)
    summed = everyones_sum(pieces).reshape(-1, hid)
    swapped = exchange(summed, "view", 1)
    grad_first = jnp.where(view[0] == 0, summed, swapped)
    grad_second = jnp.where(view[0] == 0, swapped, summed)
    return (loss, grad_first, grad_second)


def solution(mesh):
    placed = (
        P("dom", None),
        P("view", None),
        P(),
        P(),
        P("view", "dom", None, None),
        P("view", "dom", None),
        P("dom", None, None),
        P("dom", None),
        P("dom", None, None),
    )
    return jax.shard_map(
        per_device,
        mesh=mesh,
        in_specs=placed,
        out_specs=(P("view", "dom"), P(), P()),
        check_vma=False,
    )
```

```python
import math

import jax
import jax.numpy as jnp
from jax import lax
from jax.experimental import pallas as pl
from jax.experimental.pallas import tpu as pltpu
from jax.sharding import PartitionSpec as P


inv_temp = 5.0
norm_eps = 1e-06
BF = jnp.bfloat16
F32 = jnp.float32
LANES = 128
SLACK = 6 * 2**20


def exchange(array, axis, distance):
    return lax.ppermute(array, axis, [(i, i ^ distance) for i in range(lax.axis_size(axis))])


def index_stages():
    stages = []
    done = 1
    while done < lax.axis_size("dom"):
        ways = 4 if lax.axis_size("dom") // done % 4 == 0 else 2
        stages.append(("dom", ways, done))
        done *= ways
    return stages


def everyones_sum(pieces):
    stages = index_stages()
    for axis, ways, stride in stages:
        mine = lax.axis_index(axis) // stride % ways
        split = pieces.reshape((ways, pieces.shape[0] // ways) + pieces.shape[1:])
        arrived = [
            exchange(lax.dynamic_index_in_dim(split, mine ^ d, 0, False), axis, d * stride)
            for d in range(ways - 1, 0, -1)
        ]
        pieces = lax.dynamic_index_in_dim(split, mine, 0, False)
        for term in arrived:
            pieces = pieces + term
    for axis, ways, stride in stages[::-1]:
        mine = lax.axis_index(axis) // stride % ways
        held = [pieces] + [exchange(pieces, axis, d * stride) for d in range(1, ways)]
        ordered = []
        for j in range(ways):
            value = held[0]
            for d in range(1, ways):
                value = jnp.where(mine ^ j == d, held[d], value)
            ordered.append(value)
        pieces = jnp.concatenate(ordered, 0)
    return pieces


def to_others(rows, *live):
    parts = lax.axis_size("dom")
    rows, live = lax.optimization_barrier((rows, live))
    split = rows.reshape(parts, rows.shape[0] // parts, rows.shape[1])
    moved = lax.all_to_all(split, "dom", split_axis=0, concat_axis=0, tiled=True)
    moved, live = lax.optimization_barrier((moved, live))
    return moved.reshape(rows.shape), *live


def kernel_call(body, outs, args, scratch=(), scalars=0, flops=0, space=pltpu.VMEM):
    moved = sum(a.size * a.dtype.itemsize for a in tuple(args) + tuple(outs))
    held = sum(math.prod(a.shape) * 4 for a in scratch)
    return pl.pallas_call(
        body,
        out_shape=tuple(jax.ShapeDtypeStruct(o.shape, o.dtype) for o in outs),
        in_specs=[pl.BlockSpec(memory_space=pltpu.SMEM)] * scalars
        + [pl.BlockSpec(memory_space=space)] * (len(args) - scalars),
        out_specs=tuple(pl.BlockSpec(memory_space=pltpu.VMEM) for _ in outs),
        scratch_shapes=list(scratch),
        cost_estimate=pl.CostEstimate(flops=flops, bytes_accessed=moved, transcendentals=0),
        compiler_params=pltpu.CompilerParams(vmem_limit_bytes=moved + held + SLACK),
        name=body.__name__ if hasattr(body, "__name__") else body.func.__name__,
    )(*(pltpu.with_memory_space_constraint(a, pltpu.HBM) if space == pltpu.HBM else a for a in args))


def shape(rows, cols, dtype):
    return jax.ShapeDtypeStruct((rows, cols), dtype)


def dot(a, b, dims=((1,), (0,))):
    return lax.dot_general(a, b, (dims, ((), ())), preferred_element_type=F32)


def pick_matrix(slots_ref, live_ref, place, width):
    cap, parts = slots_ref.shape

    @pl.loop(0, parts)
    def _(r):
        rows = lax.broadcasted_iota(jnp.int32, (cap, LANES), 0)
        slots = jnp.full((cap, LANES), -1, jnp.int32)
        for c in range(cap):
            slot = slots_ref[c, r]
            if live_ref is not None:
                slot = jnp.where(c < live_ref[0, r], slot, -1)
            slots = jnp.where(rows == c, slot, slots)
        place[rows_at(r, cap), :] = slots

    slots = place[...]
    lanes = lax.broadcasted_iota(jnp.int32, slots.shape, 1)
    columns = [
        jnp.where(slots == lanes + first, 1.0, 0.0).astype(BF) for first in range(0, width, LANES)
    ]
    return jnp.concatenate(columns, axis=1)


def wide(column, width):
    return jnp.concatenate([column] * (width // LANES), axis=1)


def rows_at(index, size):
    return pl.ds(pl.multiple_of(index * size, size), size)


def prepare(
    slots_hbm, live_hbm, picks_hbm, feat_hbm, keep_hbm, tiles_hbm, first_hbm, second_hbm, src_hbm,
    out_ref, send_ref, pick_ref, masked_ref, tiles_ref, first_ref, second_ref, src_ref,
    slots, live, picks, feat, keep, place, sems
):
    pairs = [
        (slots_hbm, slots), (live_hbm, live), (feat_hbm, feat), (keep_hbm, keep),
        (picks_hbm, picks), (src_hbm, src_ref), (tiles_hbm, tiles_ref), (first_hbm, first_ref),
        (second_hbm, second_ref),
    ]
    copies = [pltpu.make_async_copy(a, b, sems.at[k]) for k, (a, b) in enumerate(pairs)]
    for copy in copies:
        copy.start()
    copies[0].wait()
    copies[1].wait()
    send_ref[...] = pick_matrix(slots, live, place, feat.shape[0])
    copies[2].wait()
    copies[3].wait()
    masked = feat[...] * keep[...].astype(F32).astype(BF)
    masked_ref[...] = masked
    out_ref[...] = dot(send_ref[...], masked).astype(BF)
    copies[4].wait()
    pick_ref[...] = pick_matrix(picks, None, place, feat.shape[0])
    for copy in copies[5:]:
        copy.wait()


def tile_row(tiles_ref, b, tpb):
    return jnp.concatenate([tiles_ref[b * tpb + t] for t in range(tpb)], axis=1)


def mixed_sum(src_ref, tiles, ext, b, bs):
    picked = [ext[rows_at(src_ref[b, t], bs), :] for t in range(src_ref.shape[1])]
    return dot(tiles, jnp.concatenate(picked, axis=0)) + ext[rows_at(b, bs), :].astype(F32)


def first_layer(
    src_ref, masked_ref, halo_ref, tiles_ref, w_ref, send_ref,
    mixed_ref, alive_ref, hidden_ref, inv_ref, out_ref, ext
):
    blocks, tpb = src_ref.shape
    bs = tiles_ref.shape[1]
    rows, width = masked_ref.shape
    ext[:rows, :] = masked_ref[...]
    ext[rows:, :] = halo_ref[...]

    @pl.loop(0, blocks)
    def _(b):
        here = rows_at(b, bs)
        tiles = tile_row(tiles_ref, b, tpb)
        inv = 1.0 / (1.0 + dot(tiles, jnp.ones((tpb * bs, LANES), BF)))
        inv_ref[here, :] = inv
        mixed_ref[here, :] = (mixed_sum(src_ref, tiles, ext, b, bs) * wide(inv, width)).astype(BF)

    step = rows // 4

    @pl.loop(0, 4)
    def _(c):
        here = rows_at(c, step)
        pre = dot(mixed_ref[here, :], w_ref[...])
        alive_ref[here, :] = jnp.where(pre > 0, 1.0, 0.0).astype(BF)
        hidden_ref[here, :] = jnp.maximum(pre, 0.0).astype(BF)

    out_ref[...] = dot(send_ref[...], hidden_ref[...]).astype(BF)


def second_layer(
    src_ref, hidden_ref, halo_ref, tiles_ref, inv_ref, w_ref, pick_ref,
    mixed_ref, normed_ref, scale_ref, unit_ref, out_ref, ext
):
    blocks, tpb = src_ref.shape
    bs = tiles_ref.shape[1]
    rows, width = hidden_ref.shape
    ext[:rows, :] = hidden_ref[...]
    ext[rows:, :] = halo_ref[...]

    @pl.loop(0, blocks)
    def _(b):
        here = rows_at(b, bs)
        total = mixed_sum(src_ref, tile_row(tiles_ref, b, tpb), ext, b, bs)
        mixed_ref[here, :] = (total * wide(inv_ref[here, :], width)).astype(BF)

    step = rows // 4

    @pl.loop(0, 4)
    def _(c):
        here = rows_at(c, step)
        projected = dot(mixed_ref[here, :], w_ref[...])
        scale = lax.rsqrt(jnp.sum(projected * projected, axis=1, keepdims=True) + norm_eps)
        normed = projected * scale
        normed_ref[here, :] = normed
        scale_ref[here, :] = jnp.broadcast_to(scale, (step, LANES))
        unit_ref[here, :] = normed.astype(BF)

    out_ref[...] = dot(pick_ref[...], unit_ref[...]).astype(BF)


def soft_terms(anchor, negatives, positive):
    expo = jnp.exp(inv_temp * dot(anchor, negatives, ((1,), (1,))))
    top = jnp.exp(positive)
    total = top + jnp.sum(expo, axis=1, keepdims=True)
    return (expo / total).astype(BF), top / total - 1.0, total


def contrast_other(unit_ref, other_ref, neg_ref, share_ref, positive_ref, grad_ref):
    rows = unit_ref.shape[0]
    step = rows // 4
    grad_ref[...] = jnp.zeros_like(grad_ref)

    @pl.loop(0, 4)
    def _(c):
        here = rows_at(c, step)
        other = other_ref[here, :]
        product = unit_ref[here, :].astype(F32) * other.astype(F32)
        positive = inv_temp * jnp.sum(product, axis=1, keepdims=True)
        prob, share, _ = soft_terms(other, neg_ref[...], positive)
        share_ref[here, :] = jnp.broadcast_to(share, (step, LANES))
        positive_ref[here, :] = jnp.broadcast_to(positive, (step, LANES))
        grad_ref[...] += inv_temp * dot(prob, other, ((0,), (0,)))


def backward(
    src_ref, tiles_ref, unit_ref, other_ref, neg_ref, share_ref, positive_ref, back_ref, pick_ref,
    normed_ref, scale_ref, w_ref, inv_ref, mixed_ref,
    loss_ref, own_ref, out_ref, grad_ref, terms, proj_ref, scaled_ref, total
):
    blocks, tpb = src_ref.shape
    bs = tiles_ref.shape[1]
    rows, width = unit_ref.shape
    count = back_ref.shape[0]
    left = back_ref[...]
    for k in range(3):
        term = left.astype(BF)
        terms[k * count : (k + 1) * count, :] = term
        left = left - term.astype(F32)
    step = rows // 4

    @pl.loop(0, 4)
    def _(c):
        here = rows_at(c, step)
        positive = positive_ref[here, :][:, :1]
        prob, share, whole = soft_terms(unit_ref[here, :], neg_ref[...], positive)
        loss_ref[here, :] = jnp.broadcast_to(jnp.log(whole) - positive, (step, LANES))
        other = other_ref[here, :].astype(F32)
        anchor = share * other + dot(prob, neg_ref[...])
        partner = wide(share_ref[here, :], width) * other
        put = pick_ref[:, here]
        came = dot(jnp.concatenate([put] * 3, axis=0), terms[...], ((0,), (0,)))
        grad = inv_temp * anchor + (inv_temp * partner + came)
        normed = normed_ref[here, :]
        inner = jnp.sum(normed * grad, axis=1, keepdims=True)
        proj = ((grad - normed * inner) * wide(scale_ref[here, :], width)).astype(BF)
        proj_ref[here, :] = proj
        mixed = dot(proj, w_ref[...], ((1,), (1,)))
        scaled = (mixed * wide(inv_ref[here, :], width)).astype(BF)
        scaled_ref[here, :] = scaled
        total[here, :] = scaled.astype(F32)

    total[rows:, :] = jnp.zeros_like(total[rows:, :])

    @pl.loop(0, blocks)
    def _(b):
        grad = scaled_ref[rows_at(b, bs), :]
        for t in range(tpb):
            there = rows_at(src_ref[b, t], bs)
            total[there, :] += dot(tiles_ref[b * tpb + t], grad, ((0,), (0,)))

    own_ref[...] = total[:rows, :]
    out_ref[...] = total[rows:, :].astype(BF)
    grad_ref[...] = dot(mixed_ref[...], proj_ref[...], ((0,), (0,)))


def finish(view_ref, own_ref, back_ref, send_ref, alive_ref, mixed_ref, second_ref, keep_ref, give_ref, grads):
    rows = own_ref.shape[0]
    step = rows // 4

    @pl.loop(0, 4)
    def _(c):
        here = rows_at(c, step)
        grad = own_ref[here, :] + dot(send_ref[:, here], back_ref[...], ((0,), (0,)))
        grads[here, :] = jnp.where(alive_ref[here, :].astype(F32) > 0, grad, 0.0).astype(BF)

    first = dot(mixed_ref[...], grads[...], ((0,), (0,)))
    view = view_ref[0]

    @pl.when(view == 0)
    def _():
        keep_ref[...] = first
        give_ref[...] = second_ref[...]

    @pl.when(view != 0)
    def _():
        keep_ref[...] = second_ref[...]
        give_ref[...] = first


def per_device(
    features, feat_keep, w_first, w_second, adjacency, tile_src, halo_rows, halo_live, neg_pick
):
    rows, feat = features.shape
    hid = w_first.shape[1]
    bs = adjacency.shape[2]
    blocks, tpb = tile_src.shape[1:]
    parts = lax.axis_size("dom")
    slots = parts * halo_rows.shape[2]
    picks = parts * neg_pick.shape[2]
    mix_flops = 2 * blocks * tpb * bs * bs * hid
    dense_flops = 2 * rows * feat * hid

    halo_slots = jnp.swapaxes(halo_rows, 1, 2)[0]
    neg_slots = jnp.swapaxes(neg_pick, 1, 2)[0]
    view = lax.axis_index("view").reshape(1)
    outgoing, send, pick, masked, tiles, w_first, w_second, src = kernel_call(
        prepare,
        [shape(slots, feat, BF), shape(slots, rows, BF), shape(picks, rows, BF), features,
         adjacency[0], w_first, w_second, tile_src[0]],
        [halo_slots, halo_live, neg_slots, features, feat_keep, adjacency[0], w_first, w_second,
         tile_src[0]],
        [pltpu.SMEM(halo_slots.shape, jnp.int32), pltpu.SMEM(halo_live.shape, jnp.int32),
         pltpu.SMEM(neg_slots.shape, jnp.int32), pltpu.VMEM(features.shape, BF),
         pltpu.VMEM(feat_keep.shape, jnp.int32), pltpu.VMEM((max(slots, picks), LANES), jnp.int32),
         pltpu.SemaphoreType.DMA((9,))],
        space=pltpu.HBM,
    )
    incoming, send, pick, masked, tiles, w_first, w_second, src, view = to_others(
        outgoing, send, pick, masked, tiles, w_first, w_second, src, view
    )
    mixed_first, alive, hidden, inv_deg, outgoing = kernel_call(
        first_layer,
        [shape(rows, feat, BF), shape(rows, hid, BF), shape(rows, hid, BF), shape(rows, LANES, F32),
         shape(slots, hid, BF)],
        [src, masked, incoming, tiles, w_first, send],
        [pltpu.VMEM((rows + slots, feat), BF)],
        scalars=1, flops=mix_flops + dense_flops,
    )
    incoming, hidden, inv_deg, pick = to_others(outgoing, hidden, inv_deg, pick)
    mixed_second, normed, scale, unit, outgoing = kernel_call(
        second_layer,
        [shape(rows, hid, BF), shape(rows, hid, F32), shape(rows, LANES, F32), shape(rows, hid, BF),
         shape(picks, hid, BF)],
        [src, hidden, incoming, tiles, inv_deg, w_second, pick],
        [pltpu.VMEM((rows + slots, hid), BF)], scalars=1, flops=mix_flops + dense_flops,
    )
    other = exchange(unit, "view", 1)
    neg_other, unit = to_others(outgoing, unit)
    neg_own = exchange(neg_other, "view", 1)
    share, positive, grad_neg = kernel_call(
        contrast_other,
        [shape(rows, LANES, F32), shape(rows, LANES, F32), shape(picks, hid, F32)],
        [unit, other, neg_other],
    )
    returned, neg_own, share, positive, unit, other = to_others(
        grad_neg, neg_own, share, positive, unit, other
    )
    loss, own, outgoing, grad_second = kernel_call(
        backward,
        [shape(rows, LANES, F32), shape(rows, hid, F32), shape(slots, hid, BF), shape(hid, hid, F32)],
        [src, tiles, unit, other, neg_own, share, positive, returned, pick, normed, scale,
         w_second, inv_deg, mixed_second],
        [pltpu.VMEM((3 * picks, hid), BF), pltpu.VMEM((rows, hid), BF), pltpu.VMEM((rows, hid), BF),
         pltpu.VMEM((rows + slots, hid), F32)],
        scalars=1, flops=mix_flops + 2 * dense_flops,
    )
    loss = loss[:, 0][None, :]
    returned, own, grad_second, view, loss = to_others(outgoing, own, grad_second, view, loss)
    kept, given = kernel_call(
        finish, [shape(hid, hid, F32), shape(hid, hid, F32)],
        [view, own, returned, send, alive, mixed_first, grad_second],
        [pltpu.VMEM((rows, hid), BF)], scalars=1, flops=dense_flops,
    )
    pieces = (kept + exchange(given, "view", 1)).reshape(parts, -1, hid)
    summed = everyones_sum(pieces).reshape(-1, hid)
    swapped = exchange(summed, "view", 1)
    grad_first = jnp.where(view[0] == 0, summed, swapped)
    grad_second = jnp.where(view[0] == 0, swapped, summed)
    return (loss, grad_first, grad_second)


def solution(mesh):
    placed = (
        P("dom", None),
        P("view", None),
        P(),
        P(),
        P("view", "dom", None, None),
        P("view", "dom", None),
        P("dom", None, None),
        P("dom", None),
        P("dom", None, None),
    )
    return jax.shard_map(
        per_device,
        mesh=mesh,
        in_specs=placed,
        out_specs=(P("view", "dom"), P(), P()),
        check_vma=False,
    )
```

```python
import math

import jax
import jax.numpy as jnp
from jax import lax
from jax.experimental import pallas as pl
from jax.experimental.pallas import tpu as pltpu
from jax.sharding import PartitionSpec as P


inv_temp = 5.0
norm_eps = 1e-06
BF = jnp.bfloat16
F32 = jnp.float32
LANES = 128
SLACK = 6 * 2**20


def exchange(array, axis, distance):
    return lax.ppermute(array, axis, [(i, i ^ distance) for i in range(lax.axis_size(axis))])


def index_stages():
    stages = []
    done = 1
    while done < lax.axis_size("dom"):
        ways = 4 if lax.axis_size("dom") // done % 4 == 0 else 2
        stages.append(("dom", ways, done))
        done *= ways
    return stages


def everyones_sum(pieces):
    stages = index_stages()
    for axis, ways, stride in stages:
        mine = lax.axis_index(axis) // stride % ways
        split = pieces.reshape((ways, pieces.shape[0] // ways) + pieces.shape[1:])
        arrived = [
            exchange(lax.dynamic_index_in_dim(split, mine ^ d, 0, False), axis, d * stride)
            for d in range(ways - 1, 0, -1)
        ]
        pieces = lax.dynamic_index_in_dim(split, mine, 0, False)
        for term in arrived:
            pieces = pieces + term
    for axis, ways, stride in stages[::-1]:
        mine = lax.axis_index(axis) // stride % ways
        held = [pieces] + [exchange(pieces, axis, d * stride) for d in range(1, ways)]
        ordered = []
        for j in range(ways):
            value = held[0]
            for d in range(1, ways):
                value = jnp.where(mine ^ j == d, held[d], value)
            ordered.append(value)
        pieces = jnp.concatenate(ordered, 0)
    return pieces


def to_others(rows, *live):
    parts = lax.axis_size("dom")
    rows, live = lax.optimization_barrier((rows, live))
    split = rows.reshape(parts, rows.shape[0] // parts, rows.shape[1])
    moved = lax.all_to_all(split, "dom", split_axis=0, concat_axis=0, tiled=True)
    moved, live = lax.optimization_barrier((moved, live))
    return moved.reshape(rows.shape), *live


def kernel_call(body, outs, args, scratch=(), scalars=0, flops=0, space=pltpu.VMEM):
    moved = sum(a.size * a.dtype.itemsize for a in tuple(args) + tuple(outs))
    held = sum(math.prod(a.shape) * 4 for a in scratch)
    return pl.pallas_call(
        body,
        out_shape=tuple(jax.ShapeDtypeStruct(o.shape, o.dtype) for o in outs),
        in_specs=[pl.BlockSpec(memory_space=pltpu.SMEM)] * scalars
        + [pl.BlockSpec(memory_space=space)] * (len(args) - scalars),
        out_specs=tuple(pl.BlockSpec(memory_space=pltpu.VMEM) for _ in outs),
        scratch_shapes=list(scratch),
        cost_estimate=pl.CostEstimate(flops=flops, bytes_accessed=moved, transcendentals=0),
        compiler_params=pltpu.CompilerParams(vmem_limit_bytes=moved + held + SLACK),
        name=body.__name__ if hasattr(body, "__name__") else body.func.__name__,
    )(*(pltpu.with_memory_space_constraint(a, pltpu.HBM) if space == pltpu.HBM else a for a in args))


def shape(rows, cols, dtype):
    return jax.ShapeDtypeStruct((rows, cols), dtype)


def dot(a, b, dims=((1,), (0,))):
    return lax.dot_general(a, b, (dims, ((), ())), preferred_element_type=F32)


def pick_matrix(slots_ref, live_ref, place, width):
    cap, parts = slots_ref.shape

    @pl.loop(0, parts)
    def _(r):
        rows = lax.broadcasted_iota(jnp.int32, (cap, LANES), 0)
        slots = jnp.full((cap, LANES), -1, jnp.int32)
        for c in range(cap):
            slot = slots_ref[c, r]
            if live_ref is not None:
                slot = jnp.where(c < live_ref[0, r], slot, -1)
            slots = jnp.where(rows == c, slot, slots)
        place[rows_at(r, cap), :] = slots

    slots = place[...]
    lanes = lax.broadcasted_iota(jnp.int32, slots.shape, 1)
    columns = [
        jnp.where(slots == lanes + first, 1.0, 0.0).astype(BF) for first in range(0, width, LANES)
    ]
    return jnp.concatenate(columns, axis=1)


def wide(column, width):
    return jnp.concatenate([column] * (width // LANES), axis=1)


def rows_at(index, size):
    return pl.ds(pl.multiple_of(index * size, size), size)


def prepare(
    slots_hbm, live_hbm, picks_hbm, feat_hbm, keep_hbm, tiles_hbm, first_hbm, second_hbm, src_hbm,
    out_ref, send_ref, pick_ref, masked_ref, tiles_ref, first_ref, second_ref, src_ref,
    slots, live, picks, feat, keep, place, sems
):
    pairs = [
        (slots_hbm, slots), (live_hbm, live), (feat_hbm, feat), (keep_hbm, keep),
        (picks_hbm, picks), (src_hbm, src_ref), (tiles_hbm, tiles_ref), (first_hbm, first_ref),
        (second_hbm, second_ref),
    ]
    copies = [pltpu.make_async_copy(a, b, sems.at[k]) for k, (a, b) in enumerate(pairs)]
    for copy in copies:
        copy.start()
    copies[0].wait()
    copies[1].wait()
    send_ref[...] = pick_matrix(slots, live, place, feat.shape[0])
    copies[2].wait()
    copies[3].wait()
    masked = feat[...] * keep[...].astype(F32).astype(BF)
    masked_ref[...] = masked
    out_ref[...] = dot(send_ref[...], masked).astype(BF)
    copies[4].wait()
    pick_ref[...] = pick_matrix(picks, None, place, feat.shape[0])
    for copy in copies[5:]:
        copy.wait()


def tile_row(tiles_ref, b, tpb):
    return jnp.concatenate([tiles_ref[b * tpb + t] for t in range(tpb)], axis=1)


def mixed_sum(src_ref, tiles, ext, b, bs):
    picked = [ext[rows_at(src_ref[b, t], bs), :] for t in range(src_ref.shape[1])]
    return dot(tiles, jnp.concatenate(picked, axis=0)) + ext[rows_at(b, bs), :].astype(F32)


def first_layer(
    src_ref, masked_ref, halo_ref, tiles_ref, w_ref, send_ref,
    mixed_ref, alive_ref, hidden_ref, inv_ref, out_ref, ext
):
    blocks, tpb = src_ref.shape
    bs = tiles_ref.shape[1]
    rows, width = masked_ref.shape
    ext[:rows, :] = masked_ref[...]
    ext[rows:, :] = halo_ref[...]

    @pl.loop(0, blocks, unroll=True)
    def _(b):
        here = rows_at(b, bs)
        tiles = tile_row(tiles_ref, b, tpb)
        inv = 1.0 / (1.0 + dot(tiles, jnp.ones((tpb * bs, LANES), BF)))
        inv_ref[here, :] = inv
        mixed_ref[here, :] = (mixed_sum(src_ref, tiles, ext, b, bs) * wide(inv, width)).astype(BF)

    step = rows // 4

    @pl.loop(0, 4, unroll=True)
    def _(c):
        here = rows_at(c, step)
        pre = dot(mixed_ref[here, :], w_ref[...])
        alive_ref[here, :] = jnp.where(pre > 0, 1.0, 0.0).astype(BF)
        hidden_ref[here, :] = jnp.maximum(pre, 0.0).astype(BF)

    out_ref[...] = dot(send_ref[...], hidden_ref[...]).astype(BF)


def second_layer(
    src_ref, hidden_ref, halo_ref, tiles_ref, inv_ref, w_ref, pick_ref,
    mixed_ref, normed_ref, scale_ref, unit_ref, out_ref, ext
):
    blocks, tpb = src_ref.shape
    bs = tiles_ref.shape[1]
    rows, width = hidden_ref.shape
    ext[:rows, :] = hidden_ref[...]
    ext[rows:, :] = halo_ref[...]

    @pl.loop(0, blocks, unroll=True)
    def _(b):
        here = rows_at(b, bs)
        total = mixed_sum(src_ref, tile_row(tiles_ref, b, tpb), ext, b, bs)
        mixed_ref[here, :] = (total * wide(inv_ref[here, :], width)).astype(BF)

    step = rows // 4

    @pl.loop(0, 4, unroll=True)
    def _(c):
        here = rows_at(c, step)
        projected = dot(mixed_ref[here, :], w_ref[...])
        scale = lax.rsqrt(jnp.sum(projected * projected, axis=1, keepdims=True) + norm_eps)
        normed = projected * scale
        normed_ref[here, :] = normed
        scale_ref[here, :] = jnp.broadcast_to(scale, (step, LANES))
        unit_ref[here, :] = normed.astype(BF)

    out_ref[...] = dot(pick_ref[...], unit_ref[...]).astype(BF)


def soft_terms(anchor, negatives, positive):
    expo = jnp.exp(inv_temp * dot(anchor, negatives, ((1,), (1,))))
    top = jnp.exp(positive)
    total = top + jnp.sum(expo, axis=1, keepdims=True)
    return (expo / total).astype(BF), top / total - 1.0, total


def contrast_other(unit_ref, other_ref, neg_ref, share_ref, positive_ref, out_ref, grad_ref):
    rows = unit_ref.shape[0]
    step = rows // 4
    grad_ref[...] = jnp.zeros_like(grad_ref)

    @pl.loop(0, 4, unroll=True)
    def _(c):
        here = rows_at(c, step)
        other = other_ref[here, :]
        product = unit_ref[here, :].astype(F32) * other.astype(F32)
        positive = inv_temp * jnp.sum(product, axis=1, keepdims=True)
        prob, share, _ = soft_terms(other, neg_ref[...], positive)
        share_ref[here, :] = jnp.broadcast_to(share, (step, LANES))
        positive_ref[here, :] = jnp.broadcast_to(positive, (step, LANES))
        grad_ref[...] += inv_temp * dot(prob, other, ((0,), (0,)))

    grad = grad_ref[...]
    rows_sent = neg_ref[...].astype(F32)
    along = jnp.sum(grad * rows_sent, axis=1, keepdims=True)
    width = grad.shape[1]
    out_ref[:, :width] = (grad - along * rows_sent).astype(BF)
    lanes = lax.broadcasted_iota(jnp.int32, (grad.shape[0], LANES), 1)
    left = jnp.broadcast_to(along, lanes.shape)
    terms = jnp.zeros_like(left)
    for k in range(3):
        term = left.astype(BF).astype(F32)
        terms = jnp.where(lanes == k, term, terms)
        left = left - term
    out_ref[:, width:] = terms.astype(BF)


def backward(
    unit_ref, other_ref, neg_ref, share_ref, positive_ref, back_ref, pick_ref,
    normed_ref, scale_ref, w_ref, inv_ref, mixed_ref,
    loss_ref, scaled_ref, grad_ref, proj_ref
):
    rows, width = unit_ref.shape
    step = rows // 4

    @pl.loop(0, 4, unroll=True)
    def _(c):
        here = rows_at(c, step)
        positive = positive_ref[here, :][:, :1]
        unit = unit_ref[here, :]
        prob, share, whole = soft_terms(unit, neg_ref[...], positive)
        loss = jnp.broadcast_to(jnp.log(whole) - positive, (step, LANES))
        loss_ref[:, here] = jnp.transpose(loss)[:1, :]
        other = other_ref[here, :].astype(F32)
        came = dot(pick_ref[:, here], back_ref[...], ((0,), (0,)))
        along = jnp.sum(came[:, width:], axis=1, keepdims=True)
        weight = inv_temp * share + inv_temp * share_ref[here, :][:, :1]
        grad = weight * other + inv_temp * dot(prob, neg_ref[...])
        grad = grad + (came[:, :width] + along * unit.astype(F32))
        normed = normed_ref[here, :]
        inner = jnp.sum(normed * grad, axis=1, keepdims=True)
        proj = ((grad - normed * inner) * wide(scale_ref[here, :], width)).astype(BF)
        proj_ref[here, :] = proj
        mixed = dot(proj, w_ref[...], ((1,), (1,)))
        scaled_ref[here, :] = (mixed * wide(inv_ref[here, :], width)).astype(BF)

    grad_ref[...] = dot(mixed_ref[...], proj_ref[...], ((0,), (0,)))


def mix_back(src_ref, tiles_ref, scaled_ref, own_ref, out_ref, total):
    blocks, tpb = src_ref.shape
    bs = tiles_ref.shape[1]
    rows = scaled_ref.shape[0]
    total[:rows, :] = scaled_ref[...].astype(F32)
    total[rows:, :] = jnp.zeros_like(total[rows:, :])

    @pl.loop(0, blocks, unroll=True)
    def _(b):
        spread = dot(tile_row(tiles_ref, b, tpb), scaled_ref[rows_at(b, bs), :], ((0,), (0,)))
        for t in range(tpb):
            total[rows_at(src_ref[b, t], bs), :] += spread[t * bs : (t + 1) * bs, :]

    own_ref[...] = total[:rows, :]
    out_ref[...] = total[rows:, :].astype(BF)


def finish(view_ref, own_ref, back_ref, send_ref, alive_ref, mixed_ref, second_ref, keep_ref, give_ref, grads):
    rows = own_ref.shape[0]
    step = rows // 4

    @pl.loop(0, 4, unroll=True)
    def _(c):
        here = rows_at(c, step)
        grad = own_ref[here, :] + dot(send_ref[:, here], back_ref[...], ((0,), (0,)))
        grads[here, :] = jnp.where(alive_ref[here, :].astype(F32) > 0, grad, 0.0).astype(BF)

    first = dot(mixed_ref[...], grads[...], ((0,), (0,)))
    view = view_ref[0]

    @pl.when(view == 0)
    def _():
        keep_ref[...] = first
        give_ref[...] = second_ref[...]

    @pl.when(view != 0)
    def _():
        keep_ref[...] = second_ref[...]
        give_ref[...] = first


def per_device(
    features, feat_keep, w_first, w_second, adjacency, tile_src, halo_rows, halo_live, neg_pick
):
    rows, feat = features.shape
    hid = w_first.shape[1]
    bs = adjacency.shape[2]
    blocks, tpb = tile_src.shape[1:]
    parts = lax.axis_size("dom")
    slots = parts * halo_rows.shape[2]
    picks = parts * neg_pick.shape[2]
    mix_flops = 2 * blocks * tpb * bs * bs * hid
    dense_flops = 2 * rows * feat * hid

    halo_slots = jnp.swapaxes(halo_rows, 1, 2)[0]
    neg_slots = jnp.swapaxes(neg_pick, 1, 2)[0]
    view = lax.axis_index("view").reshape(1)
    outgoing, send, pick, masked, tiles, w_first, w_second, src = kernel_call(
        prepare,
        [shape(slots, feat, BF), shape(slots, rows, BF), shape(picks, rows, BF), features,
         adjacency[0], w_first, w_second, tile_src[0]],
        [halo_slots, halo_live, neg_slots, features, feat_keep, adjacency[0], w_first, w_second,
         tile_src[0]],
        [pltpu.SMEM(halo_slots.shape, jnp.int32), pltpu.SMEM(halo_live.shape, jnp.int32),
         pltpu.SMEM(neg_slots.shape, jnp.int32), pltpu.VMEM(features.shape, BF),
         pltpu.VMEM(feat_keep.shape, jnp.int32), pltpu.VMEM((max(slots, picks), LANES), jnp.int32),
         pltpu.SemaphoreType.DMA((9,))],
        space=pltpu.HBM,
    )
    incoming, send, pick, masked, tiles, w_first, w_second, src, view = to_others(
        outgoing, send, pick, masked, tiles, w_first, w_second, src, view
    )
    mixed_first, alive, hidden, inv_deg, outgoing = kernel_call(
        first_layer,
        [shape(rows, feat, BF), shape(rows, hid, BF), shape(rows, hid, BF), shape(rows, LANES, F32),
         shape(slots, hid, BF)],
        [src, masked, incoming, tiles, w_first, send],
        [pltpu.VMEM((rows + slots, feat), BF)],
        scalars=1, flops=mix_flops + dense_flops,
    )
    incoming, hidden, inv_deg, pick = to_others(outgoing, hidden, inv_deg, pick)
    mixed_second, normed, scale, unit, outgoing = kernel_call(
        second_layer,
        [shape(rows, hid, BF), shape(rows, hid, F32), shape(rows, LANES, F32), shape(rows, hid, BF),
         shape(picks, hid, BF)],
        [src, hidden, incoming, tiles, inv_deg, w_second, pick],
        [pltpu.VMEM((rows + slots, hid), BF)], scalars=1, flops=mix_flops + dense_flops,
    )
    other = exchange(unit, "view", 1)
    neg_other, unit = to_others(outgoing, unit)
    neg_own = exchange(neg_other, "view", 1)
    share, positive, grad_neg = kernel_call(
        contrast_other,
        [shape(rows, LANES, F32), shape(rows, LANES, F32), shape(picks, hid + LANES, BF)],
        [unit, other, neg_other], [pltpu.VMEM((picks, hid), F32)],
    )
    returned, neg_own, share, positive, unit, other = to_others(
        grad_neg, neg_own, share, positive, unit, other
    )
    loss, scaled, grad_second = kernel_call(
        backward,
        [shape(1, rows, F32), shape(rows, hid, BF), shape(hid, hid, F32)],
        [unit, other, neg_own, share, positive, returned, pick, normed, scale,
         w_second, inv_deg, mixed_second],
        [pltpu.VMEM((rows, hid), BF)], flops=2 * dense_flops,
    )
    own, outgoing = kernel_call(
        mix_back, [shape(rows, hid, F32), shape(slots, hid, BF)], [src, tiles, scaled],
        [pltpu.VMEM((rows + slots, hid), F32)], scalars=1, flops=mix_flops,
    )
    returned, own, grad_second, view, loss = to_others(outgoing, own, grad_second, view, loss)
    kept, given = kernel_call(
        finish, [shape(hid, hid, F32), shape(hid, hid, F32)],
        [view, own, returned, send, alive, mixed_first, grad_second],
        [pltpu.VMEM((rows, hid), BF)], scalars=1, flops=dense_flops,
    )
    pieces = (kept + exchange(given, "view", 1)).reshape(parts, -1, hid)
    summed = everyones_sum(pieces).reshape(-1, hid)
    swapped = exchange(summed, "view", 1)
    grad_first = jnp.where(view[0] == 0, summed, swapped)
    grad_second = jnp.where(view[0] == 0, swapped, summed)
    return (loss, grad_first, grad_second)


def solution(mesh):
    placed = (
        P("dom", None),
        P("view", None),
        P(),
        P(),
        P("view", "dom", None, None),
        P("view", "dom", None),
        P("dom", None, None),
        P("dom", None),
        P("dom", None, None),
    )
    return jax.shard_map(
        per_device,
        mesh=mesh,
        in_specs=placed,
        out_specs=(P("view", "dom"), P(), P()),
        check_vma=False,
    )
```

```python
import math

import jax
import jax.numpy as jnp
from jax import lax
from jax.experimental import pallas as pl
from jax.experimental.pallas import tpu as pltpu
from jax.sharding import PartitionSpec as P


inv_temp = 5.0
norm_eps = 1e-06
BF = jnp.bfloat16
F32 = jnp.float32
LANES = 128
SLACK = 6 * 2**20


def exchange(array, axis, distance):
    return lax.ppermute(array, axis, [(i, i ^ distance) for i in range(lax.axis_size(axis))])


def sum_slots():
    stages = []
    done = 1
    while done < lax.axis_size("dom"):
        ways = 4 if lax.axis_size("dom") // done % 4 == 0 else 2
        stages.append((ways, done))
        done *= ways
    turned = stages[::-1]
    if any(a[0] != b[0] for a, b in zip(stages, turned)):
        turned = stages
    return [(a[0], a[1], b[1]) for a, b in zip(stages, turned)]


def among(array, distances):
    parts = lax.axis_size("dom")
    pairs = [
        (view * parts + i, view * parts + (i ^ distances[min(view, 1)]))
        for view in range(lax.axis_size("view"))
        for i in range(parts)
    ]
    return lax.ppermute(array, ("view", "dom"), pairs)


def place_in(ways, stride, turned):
    part = lax.axis_index("dom")
    return jnp.where(lax.axis_index("view") == 0, part // stride, part // turned) % ways


def everyones_sum(pieces):
    slots = sum_slots()
    for ways, stride, turned in slots:
        mine = place_in(ways, stride, turned)
        split = pieces.reshape((ways, pieces.shape[0] // ways) + pieces.shape[1:])
        arrived = [
            among(lax.dynamic_index_in_dim(split, mine ^ d, 0, False), (d * stride, d * turned))
            for d in range(ways - 1, 0, -1)
        ]
        pieces = lax.dynamic_index_in_dim(split, mine, 0, False)
        for term in arrived:
            pieces = pieces + term
    for ways, stride, turned in slots[::-1]:
        mine = place_in(ways, stride, turned)
        held = [pieces] + [among(pieces, (d * stride, d * turned)) for d in range(1, ways)]
        ordered = []
        for j in range(ways):
            value = held[0]
            for d in range(1, ways):
                value = jnp.where(mine ^ j == d, held[d], value)
            ordered.append(value)
        pieces = jnp.concatenate(ordered, 0)
    return pieces


def to_others(rows, *live):
    parts = lax.axis_size("dom")
    rows, live = lax.optimization_barrier((rows, live))
    split = rows.reshape(parts, rows.shape[0] // parts, rows.shape[1])
    moved = lax.all_to_all(split, "dom", split_axis=0, concat_axis=0, tiled=True)
    moved, live = lax.optimization_barrier((moved, live))
    return moved.reshape(rows.shape), *live


def kernel_call(body, outs, args, scratch=(), scalars=0, flops=0, space=pltpu.VMEM):
    moved = sum(a.size * a.dtype.itemsize for a in tuple(args) + tuple(outs))
    held = sum(math.prod(a.shape) * 4 for a in scratch)
    return pl.pallas_call(
        body,
        out_shape=tuple(jax.ShapeDtypeStruct(o.shape, o.dtype) for o in outs),
        in_specs=[pl.BlockSpec(memory_space=pltpu.SMEM)] * scalars
        + [pl.BlockSpec(memory_space=space)] * (len(args) - scalars),
        out_specs=tuple(pl.BlockSpec(memory_space=pltpu.VMEM) for _ in outs),
        scratch_shapes=list(scratch),
        cost_estimate=pl.CostEstimate(flops=flops, bytes_accessed=moved, transcendentals=0),
        compiler_params=pltpu.CompilerParams(vmem_limit_bytes=moved + held + SLACK),
        name=body.__name__ if hasattr(body, "__name__") else body.func.__name__,
    )(*(pltpu.with_memory_space_constraint(a, pltpu.HBM) if space == pltpu.HBM else a for a in args))


def shape(rows, cols, dtype):
    return jax.ShapeDtypeStruct((rows, cols), dtype)


def dot(a, b, dims=((1,), (0,))):
    return lax.dot_general(a, b, (dims, ((), ())), preferred_element_type=F32)


def pick_matrix(slots_ref, live_ref, place, width):
    cap, parts = slots_ref.shape

    @pl.loop(0, parts)
    def _(r):
        rows = lax.broadcasted_iota(jnp.int32, (cap, LANES), 0)
        slots = jnp.full((cap, LANES), -1, jnp.int32)
        for c in range(cap):
            slot = slots_ref[c, r]
            if live_ref is not None:
                slot = jnp.where(c < live_ref[0, r], slot, -1)
            slots = jnp.where(rows == c, slot, slots)
        place[rows_at(r, cap), :] = slots

    slots = place[...]
    lanes = lax.broadcasted_iota(jnp.int32, slots.shape, 1)
    columns = [
        jnp.where(slots == lanes + first, 1.0, 0.0).astype(BF) for first in range(0, width, LANES)
    ]
    return jnp.concatenate(columns, axis=1)


def wide(column, width):
    return jnp.concatenate([column] * (width // LANES), axis=1)


def rows_at(index, size):
    return pl.ds(pl.multiple_of(index * size, size), size)


def prepare(
    slots_hbm, live_hbm, picks_hbm, feat_hbm, keep_hbm, tiles_hbm, first_hbm, second_hbm, src_hbm,
    out_ref, send_ref, pick_ref, masked_ref, tiles_ref, first_ref, second_ref, src_ref,
    slots, live, picks, feat, keep, place, sems
):
    pairs = [
        (slots_hbm, slots), (live_hbm, live), (feat_hbm, feat), (keep_hbm, keep),
        (picks_hbm, picks), (src_hbm, src_ref), (tiles_hbm, tiles_ref), (first_hbm, first_ref),
        (second_hbm, second_ref),
    ]
    copies = [pltpu.make_async_copy(a, b, sems.at[k]) for k, (a, b) in enumerate(pairs)]
    for copy in copies:
        copy.start()
    copies[0].wait()
    copies[1].wait()
    send_ref[...] = pick_matrix(slots, live, place, feat.shape[0])
    copies[2].wait()
    copies[3].wait()
    masked = feat[...] * keep[...].astype(F32).astype(BF)
    masked_ref[...] = masked
    out_ref[...] = dot(send_ref[...], masked).astype(BF)
    copies[4].wait()
    pick_ref[...] = pick_matrix(picks, None, place, feat.shape[0])
    for copy in copies[5:]:
        copy.wait()


def tile_row(tiles_ref, b, tpb):
    return jnp.concatenate([tiles_ref[b * tpb + t] for t in range(tpb)], axis=1)


def mixed_sum(src_ref, tiles, ext, b, bs):
    picked = [ext[rows_at(src_ref[b, t], bs), :] for t in range(src_ref.shape[1])]
    return dot(tiles, jnp.concatenate(picked, axis=0)) + ext[rows_at(b, bs), :].astype(F32)


def first_layer(
    src_ref, masked_ref, halo_ref, tiles_ref, w_ref, send_ref,
    mixed_ref, alive_ref, hidden_ref, inv_ref, out_ref, ext
):
    blocks, tpb = src_ref.shape
    bs = tiles_ref.shape[1]
    rows, width = masked_ref.shape
    ext[:rows, :] = masked_ref[...]
    ext[rows:, :] = halo_ref[...]

    @pl.loop(0, blocks, unroll=True)
    def _(b):
        here = rows_at(b, bs)
        tiles = tile_row(tiles_ref, b, tpb)
        inv = 1.0 / (1.0 + dot(tiles, jnp.ones((tpb * bs, LANES), BF)))
        inv_ref[here, :] = inv
        mixed_ref[here, :] = (mixed_sum(src_ref, tiles, ext, b, bs) * wide(inv, width)).astype(BF)

    step = rows // 4

    @pl.loop(0, 4, unroll=True)
    def _(c):
        here = rows_at(c, step)
        pre = dot(mixed_ref[here, :], w_ref[...])
        alive_ref[here, :] = jnp.where(pre > 0, 1.0, 0.0).astype(BF)
        hidden_ref[here, :] = jnp.maximum(pre, 0.0).astype(BF)

    out_ref[...] = dot(send_ref[...], hidden_ref[...]).astype(BF)


def second_layer(
    src_ref, hidden_ref, halo_ref, tiles_ref, inv_ref, w_ref, pick_ref,
    mixed_ref, normed_ref, scale_ref, unit_ref, out_ref, ext
):
    blocks, tpb = src_ref.shape
    bs = tiles_ref.shape[1]
    rows, width = hidden_ref.shape
    ext[:rows, :] = hidden_ref[...]
    ext[rows:, :] = halo_ref[...]

    @pl.loop(0, blocks, unroll=True)
    def _(b):
        here = rows_at(b, bs)
        total = mixed_sum(src_ref, tile_row(tiles_ref, b, tpb), ext, b, bs)
        mixed_ref[here, :] = (total * wide(inv_ref[here, :], width)).astype(BF)

    step = rows // 4

    @pl.loop(0, 4, unroll=True)
    def _(c):
        here = rows_at(c, step)
        projected = dot(mixed_ref[here, :], w_ref[...])
        scale = lax.rsqrt(jnp.sum(projected * projected, axis=1, keepdims=True) + norm_eps)
        normed = projected * scale
        normed_ref[here, :] = normed
        scale_ref[here, :] = jnp.broadcast_to(scale, (step, LANES))
        unit_ref[here, :] = normed.astype(BF)

    out_ref[...] = dot(pick_ref[...], unit_ref[...]).astype(BF)


def soft_terms(anchor, negatives, positive):
    expo = jnp.exp(inv_temp * dot(anchor, negatives, ((1,), (1,))))
    top = jnp.exp(positive)
    total = top + jnp.sum(expo, axis=1, keepdims=True)
    return (expo / total).astype(BF), top / total - 1.0, total


def contrast_other(unit_ref, other_ref, neg_ref, share_ref, positive_ref, out_ref, grad_ref):
    rows = unit_ref.shape[0]
    step = rows // 4
    grad_ref[...] = jnp.zeros_like(grad_ref)

    @pl.loop(0, 4)
    def _(c):
        here = rows_at(c, step)
        other = other_ref[here, :]
        product = unit_ref[here, :].astype(F32) * other.astype(F32)
        positive = inv_temp * jnp.sum(product, axis=1, keepdims=True)
        prob, share, _ = soft_terms(other, neg_ref[...], positive)
        share_ref[here, :] = jnp.broadcast_to(share, (step, LANES))
        positive_ref[here, :] = jnp.broadcast_to(positive, (step, LANES))
        grad_ref[...] += inv_temp * dot(prob, other, ((0,), (0,)))

    grad = grad_ref[...]
    rows_sent = neg_ref[...].astype(F32)
    along = jnp.sum(grad * rows_sent, axis=1, keepdims=True)
    width = grad.shape[1]
    out_ref[:, :width] = (grad - along * rows_sent).astype(BF)
    lanes = lax.broadcasted_iota(jnp.int32, (grad.shape[0], LANES), 1)
    left = jnp.broadcast_to(along, lanes.shape)
    terms = jnp.zeros_like(left)
    for k in range(3):
        term = left.astype(BF).astype(F32)
        terms = jnp.where(lanes == k, term, terms)
        left = left - term
    out_ref[:, width:] = terms.astype(BF)


def backward(
    unit_ref, other_ref, neg_ref, share_ref, positive_ref, back_ref, pick_ref,
    normed_ref, scale_ref, w_ref, inv_ref, mixed_ref,
    loss_ref, scaled_ref, grad_ref, proj_ref
):
    rows, width = unit_ref.shape
    step = rows // 4

    @pl.loop(0, 4)
    def _(c):
        here = rows_at(c, step)
        positive = positive_ref[here, :][:, :1]
        unit = unit_ref[here, :]
        prob, share, whole = soft_terms(unit, neg_ref[...], positive)
        loss = jnp.broadcast_to(jnp.log(whole) - positive, (step, LANES))
        loss_ref[:, here] = jnp.transpose(loss)[:1, :]
        other = other_ref[here, :].astype(F32)
        came = dot(pick_ref[:, here], back_ref[...], ((0,), (0,)))
        along = jnp.sum(came[:, width:], axis=1, keepdims=True)
        weight = inv_temp * share + inv_temp * share_ref[here, :][:, :1]
        grad = weight * other + inv_temp * dot(prob, neg_ref[...])
        grad = grad + (came[:, :width] + along * unit.astype(F32))
        normed = normed_ref[here, :]
        inner = jnp.sum(normed * grad, axis=1, keepdims=True)
        proj = ((grad - normed * inner) * wide(scale_ref[here, :], width)).astype(BF)
        proj_ref[here, :] = proj
        mixed = dot(proj, w_ref[...], ((1,), (1,)))
        scaled_ref[here, :] = (mixed * wide(inv_ref[here, :], width)).astype(BF)

    grad_ref[...] = dot(mixed_ref[...], proj_ref[...], ((0,), (0,)))


def mix_back(src_ref, tiles_ref, scaled_ref, own_ref, out_ref, total):
    blocks, tpb = src_ref.shape
    bs = tiles_ref.shape[1]
    rows = scaled_ref.shape[0]
    total[:rows, :] = scaled_ref[...].astype(F32)
    total[rows:, :] = jnp.zeros_like(total[rows:, :])

    @pl.loop(0, blocks, unroll=True)
    def _(b):
        spread = dot(tile_row(tiles_ref, b, tpb), scaled_ref[rows_at(b, bs), :], ((0,), (0,)))
        for t in range(tpb):
            total[rows_at(src_ref[b, t], bs), :] += spread[t * bs : (t + 1) * bs, :]

    own_ref[...] = total[:rows, :]
    out_ref[...] = total[rows:, :].astype(BF)


def finish(view_ref, own_ref, back_ref, send_ref, alive_ref, mixed_ref, second_ref, keep_ref, give_ref, grads):
    rows = own_ref.shape[0]
    step = rows // 4

    @pl.loop(0, 4, unroll=True)
    def _(c):
        here = rows_at(c, step)
        grad = own_ref[here, :] + dot(send_ref[:, here], back_ref[...], ((0,), (0,)))
        grads[here, :] = jnp.where(alive_ref[here, :].astype(F32) > 0, grad, 0.0).astype(BF)

    first = dot(mixed_ref[...], grads[...], ((0,), (0,)))
    view = view_ref[0]

    @pl.when(view == 0)
    def _():
        keep_ref[...] = first
        give_ref[...] = second_ref[...]

    @pl.when(view != 0)
    def _():
        keep_ref[...] = second_ref[...]
        give_ref[...] = first


def per_device(
    features, feat_keep, w_first, w_second, adjacency, tile_src, halo_rows, halo_live, neg_pick
):
    rows, feat = features.shape
    hid = w_first.shape[1]
    bs = adjacency.shape[2]
    blocks, tpb = tile_src.shape[1:]
    parts = lax.axis_size("dom")
    slots = parts * halo_rows.shape[2]
    picks = parts * neg_pick.shape[2]
    mix_flops = 2 * blocks * tpb * bs * bs * hid
    dense_flops = 2 * rows * feat * hid

    halo_slots = jnp.swapaxes(halo_rows, 1, 2)[0]
    neg_slots = jnp.swapaxes(neg_pick, 1, 2)[0]
    view = lax.axis_index("view").reshape(1)
    outgoing, send, pick, masked, tiles, w_first, w_second, src = kernel_call(
        prepare,
        [shape(slots, feat, BF), shape(slots, rows, BF), shape(picks, rows, BF), features,
         adjacency[0], w_first, w_second, tile_src[0]],
        [halo_slots, halo_live, neg_slots, features, feat_keep, adjacency[0], w_first, w_second,
         tile_src[0]],
        [pltpu.SMEM(halo_slots.shape, jnp.int32), pltpu.SMEM(halo_live.shape, jnp.int32),
         pltpu.SMEM(neg_slots.shape, jnp.int32), pltpu.VMEM(features.shape, BF),
         pltpu.VMEM(feat_keep.shape, jnp.int32), pltpu.VMEM((max(slots, picks), LANES), jnp.int32),
         pltpu.SemaphoreType.DMA((9,))],
        space=pltpu.HBM,
    )
    incoming, send, pick, masked, tiles, w_first, w_second, src, view = to_others(
        outgoing, send, pick, masked, tiles, w_first, w_second, src, view
    )
    mixed_first, alive, hidden, inv_deg, outgoing = kernel_call(
        first_layer,
        [shape(rows, feat, BF), shape(rows, hid, BF), shape(rows, hid, BF), shape(rows, LANES, F32),
         shape(slots, hid, BF)],
        [src, masked, incoming, tiles, w_first, send],
        [pltpu.VMEM((rows + slots, feat), BF)],
        scalars=1, flops=mix_flops + dense_flops,
    )
    incoming, hidden, inv_deg, pick = to_others(outgoing, hidden, inv_deg, pick)
    mixed_second, normed, scale, unit, outgoing = kernel_call(
        second_layer,
        [shape(rows, hid, BF), shape(rows, hid, F32), shape(rows, LANES, F32), shape(rows, hid, BF),
         shape(picks, hid, BF)],
        [src, hidden, incoming, tiles, inv_deg, w_second, pick],
        [pltpu.VMEM((rows + slots, hid), BF)], scalars=1, flops=mix_flops + dense_flops,
    )
    other = exchange(unit, "view", 1)
    neg_other, unit = to_others(outgoing, unit)
    neg_own = exchange(neg_other, "view", 1)
    share, positive, grad_neg = kernel_call(
        contrast_other,
        [shape(rows, LANES, F32), shape(rows, LANES, F32), shape(picks, hid + LANES, BF)],
        [unit, other, neg_other], [pltpu.VMEM((picks, hid), F32)],
    )
    returned, neg_own, share, positive, unit, other = to_others(
        grad_neg, neg_own, share, positive, unit, other
    )
    loss, scaled, grad_second = kernel_call(
        backward,
        [shape(1, rows, F32), shape(rows, hid, BF), shape(hid, hid, F32)],
        [unit, other, neg_own, share, positive, returned, pick, normed, scale,
         w_second, inv_deg, mixed_second],
        [pltpu.VMEM((rows, hid), BF)], flops=2 * dense_flops,
    )
    own, outgoing = kernel_call(
        mix_back, [shape(rows, hid, F32), shape(slots, hid, BF)], [src, tiles, scaled],
        [pltpu.VMEM((rows + slots, hid), F32)], scalars=1, flops=mix_flops,
    )
    returned, own, grad_second, view, loss = to_others(outgoing, own, grad_second, view, loss)
    kept, given = kernel_call(
        finish, [shape(hid, hid, F32), shape(hid, hid, F32)],
        [view, own, returned, send, alive, mixed_first, grad_second],
        [pltpu.VMEM((rows, hid), BF)], scalars=1, flops=dense_flops,
    )
    pieces = (kept + exchange(given, "view", 1)).reshape(parts, -1, hid)
    summed = everyones_sum(pieces).reshape(-1, hid)
    swapped = exchange(summed, "view", 1)
    grad_first = jnp.where(view[0] == 0, summed, swapped)
    grad_second = jnp.where(view[0] == 0, swapped, summed)
    return (loss, grad_first, grad_second)


def solution(mesh):
    placed = (
        P("dom", None),
        P("view", None),
        P(),
        P(),
        P("view", "dom", None, None),
        P("view", "dom", None),
        P("dom", None, None),
        P("dom", None),
        P("dom", None, None),
    )
    return jax.shard_map(
        per_device,
        mesh=mesh,
        in_specs=placed,
        out_specs=(P("view", "dom"), P(), P()),
        check_vma=False,
    )
```

```python
import math

import jax
import jax.numpy as jnp
from jax import lax
from jax.experimental import pallas as pl
from jax.experimental.pallas import tpu as pltpu
from jax.sharding import PartitionSpec as P


inv_temp = 5.0
norm_eps = 1e-06
BF = jnp.bfloat16
F32 = jnp.float32
LANES = 128
SLACK = 6 * 2**20


def exchange(array, axis, distance):
    return lax.ppermute(array, axis, [(i, i ^ distance) for i in range(lax.axis_size(axis))])


def sum_slots():
    stages = []
    done = 1
    while done < lax.axis_size("dom"):
        ways = 4 if lax.axis_size("dom") // done % 4 == 0 else 2
        stages.append((ways, done))
        done *= ways
    turned = stages[::-1]
    if any(a[0] != b[0] for a, b in zip(stages, turned)):
        turned = stages
    return [(a[0], a[1], b[1]) for a, b in zip(stages, turned)]


def among(array, distances):
    parts = lax.axis_size("dom")
    pairs = [
        (view * parts + i, view * parts + (i ^ distances[min(view, 1)]))
        for view in range(lax.axis_size("view"))
        for i in range(parts)
    ]
    return lax.ppermute(array, ("view", "dom"), pairs)


def place_in(ways, stride, turned):
    part = lax.axis_index("dom")
    return jnp.where(lax.axis_index("view") == 0, part // stride, part // turned) % ways


def everyones_sum(pieces):
    slots = sum_slots()
    for ways, stride, turned in slots:
        mine = place_in(ways, stride, turned)
        split = pieces.reshape((ways, pieces.shape[0] // ways) + pieces.shape[1:])
        arrived = [
            among(lax.dynamic_index_in_dim(split, mine ^ d, 0, False), (d * stride, d * turned))
            for d in range(ways - 1, 0, -1)
        ]
        pieces = lax.dynamic_index_in_dim(split, mine, 0, False)
        for term in arrived:
            pieces = pieces + term
    for ways, stride, turned in slots[::-1]:
        mine = place_in(ways, stride, turned)
        held = [pieces] + [among(pieces, (d * stride, d * turned)) for d in range(1, ways)]
        ordered = []
        for j in range(ways):
            value = held[0]
            for d in range(1, ways):
                value = jnp.where(mine ^ j == d, held[d], value)
            ordered.append(value)
        pieces = jnp.concatenate(ordered, 0)
    return pieces


def to_others(rows, *live):
    parts = lax.axis_size("dom")
    rows, live = lax.optimization_barrier((rows, live))
    split = rows.reshape(parts, rows.shape[0] // parts, rows.shape[1])
    moved = lax.all_to_all(split, "dom", split_axis=0, concat_axis=0, tiled=True)
    moved, live = lax.optimization_barrier((moved, live))
    return moved.reshape(rows.shape), *live


def kernel_call(body, outs, args, scratch=(), scalars=0, flops=0, space=pltpu.VMEM):
    moved = sum(a.size * a.dtype.itemsize for a in tuple(args) + tuple(outs))
    held = sum(math.prod(a.shape) * 4 for a in scratch)
    return pl.pallas_call(
        body,
        out_shape=tuple(jax.ShapeDtypeStruct(o.shape, o.dtype) for o in outs),
        in_specs=[pl.BlockSpec(memory_space=pltpu.SMEM)] * scalars
        + [pl.BlockSpec(memory_space=space)] * (len(args) - scalars),
        out_specs=tuple(pl.BlockSpec(memory_space=pltpu.VMEM) for _ in outs),
        scratch_shapes=list(scratch),
        cost_estimate=pl.CostEstimate(flops=flops, bytes_accessed=moved, transcendentals=0),
        compiler_params=pltpu.CompilerParams(vmem_limit_bytes=moved + held + SLACK),
        name=body.__name__ if hasattr(body, "__name__") else body.func.__name__,
    )(*(pltpu.with_memory_space_constraint(a, pltpu.HBM) if space == pltpu.HBM else a for a in args))


def shape(rows, cols, dtype):
    return jax.ShapeDtypeStruct((rows, cols), dtype)


def dot(a, b, dims=((1,), (0,))):
    return lax.dot_general(a, b, (dims, ((), ())), preferred_element_type=F32)


def pick_matrix(slots_ref, live_ref, place, width):
    cap, parts = slots_ref.shape

    @pl.loop(0, parts)
    def _(r):
        rows = lax.broadcasted_iota(jnp.int32, (cap, LANES), 0)
        slots = jnp.full((cap, LANES), -1, jnp.int32)
        for c in range(cap):
            slot = slots_ref[c, r]
            if live_ref is not None:
                slot = jnp.where(c < live_ref[0, r], slot, -1)
            slots = jnp.where(rows == c, slot, slots)
        place[rows_at(r, cap), :] = slots

    slots = place[...]
    lanes = lax.broadcasted_iota(jnp.int32, slots.shape, 1)
    columns = [
        jnp.where(slots == lanes + first, 1.0, 0.0).astype(BF) for first in range(0, width, LANES)
    ]
    return jnp.concatenate(columns, axis=1)


def wide(column, width):
    return jnp.concatenate([column] * (width // LANES), axis=1)


def rows_at(index, size):
    return pl.ds(pl.multiple_of(index * size, size), size)


def prepare(
    slots_hbm, live_hbm, picks_hbm, feat_hbm, keep_hbm, tiles_hbm, first_hbm, second_hbm, src_hbm,
    out_ref, send_ref, pick_ref, masked_ref, tiles_ref, first_ref, second_ref, src_ref,
    slots, live, picks, feat, keep, place, sems
):
    pairs = [
        (slots_hbm, slots), (live_hbm, live), (feat_hbm, feat), (keep_hbm, keep),
        (picks_hbm, picks), (src_hbm, src_ref), (tiles_hbm, tiles_ref), (first_hbm, first_ref),
        (second_hbm, second_ref),
    ]
    copies = [pltpu.make_async_copy(a, b, sems.at[k]) for k, (a, b) in enumerate(pairs)]
    for copy in copies:
        copy.start()
    copies[0].wait()
    copies[1].wait()
    send_ref[...] = pick_matrix(slots, live, place, feat.shape[0])
    copies[2].wait()
    copies[3].wait()
    masked = feat[...] * keep[...].astype(F32).astype(BF)
    masked_ref[...] = masked
    out_ref[...] = dot(send_ref[...], masked).astype(BF)
    copies[4].wait()
    pick_ref[...] = pick_matrix(picks, None, place, feat.shape[0])
    for copy in copies[5:]:
        copy.wait()


def tile_row(tiles_ref, b, tpb):
    return jnp.concatenate([tiles_ref[b * tpb + t] for t in range(tpb)], axis=1)


def mixed_sum(src_ref, tiles, ext, b, bs):
    picked = [ext[rows_at(src_ref[b, t], bs), :] for t in range(src_ref.shape[1])]
    return dot(tiles, jnp.concatenate(picked, axis=0)) + ext[rows_at(b, bs), :].astype(F32)


def first_layer(
    src_ref, masked_ref, halo_ref, tiles_ref, w_ref, send_ref,
    mixed_ref, alive_ref, hidden_ref, inv_ref, out_ref, ext
):
    blocks, tpb = src_ref.shape
    bs = tiles_ref.shape[1]
    rows, width = masked_ref.shape
    ext[:rows, :] = masked_ref[...]
    ext[rows:, :] = halo_ref[...]

    @pl.loop(0, blocks, unroll=True)
    def _(b):
        here = rows_at(b, bs)
        tiles = tile_row(tiles_ref, b, tpb)
        inv = 1.0 / (1.0 + dot(tiles, jnp.ones((tpb * bs, LANES), BF)))
        inv_ref[here, :] = inv
        mixed_ref[here, :] = (mixed_sum(src_ref, tiles, ext, b, bs) * wide(inv, width)).astype(BF)

    step = rows

    @pl.loop(0, 1)
    def _(c):
        here = rows_at(c, step)
        pre = dot(mixed_ref[here, :], w_ref[...])
        alive_ref[here, :] = jnp.where(pre > 0, 1.0, 0.0).astype(BF)
        hidden_ref[here, :] = jnp.maximum(pre, 0.0).astype(BF)

    out_ref[...] = dot(send_ref[...], hidden_ref[...]).astype(BF)


def second_layer(
    src_ref, hidden_ref, halo_ref, tiles_ref, inv_ref, w_ref, pick_ref,
    mixed_ref, normed_ref, scale_ref, unit_ref, out_ref, ext
):
    blocks, tpb = src_ref.shape
    bs = tiles_ref.shape[1]
    rows, width = hidden_ref.shape
    ext[:rows, :] = hidden_ref[...]
    ext[rows:, :] = halo_ref[...]

    @pl.loop(0, blocks, unroll=True)
    def _(b):
        here = rows_at(b, bs)
        total = mixed_sum(src_ref, tile_row(tiles_ref, b, tpb), ext, b, bs)
        mixed_ref[here, :] = (total * wide(inv_ref[here, :], width)).astype(BF)

    step = rows

    @pl.loop(0, 1)
    def _(c):
        here = rows_at(c, step)
        projected = dot(mixed_ref[here, :], w_ref[...])
        scale = lax.rsqrt(jnp.sum(projected * projected, axis=1, keepdims=True) + norm_eps)
        normed = projected * scale
        normed_ref[here, :] = normed
        scale_ref[here, :] = jnp.broadcast_to(scale, (step, LANES))
        unit_ref[here, :] = normed.astype(BF)

    out_ref[...] = dot(pick_ref[...], unit_ref[...]).astype(BF)


def soft_terms(anchor, negatives, positive):
    expo = jnp.exp(inv_temp * dot(anchor, negatives, ((1,), (1,))))
    top = jnp.exp(positive)
    total = top + jnp.sum(expo, axis=1, keepdims=True)
    return (expo / total).astype(BF), top / total - 1.0, total


def contrast_other(unit_ref, other_ref, neg_ref, share_ref, positive_ref, out_ref, grad_ref):
    rows = unit_ref.shape[0]
    step = rows
    grad_ref[...] = jnp.zeros_like(grad_ref)

    @pl.loop(0, 1)
    def _(c):
        here = rows_at(c, step)
        other = other_ref[here, :]
        product = unit_ref[here, :].astype(F32) * other.astype(F32)
        positive = inv_temp * jnp.sum(product, axis=1, keepdims=True)
        prob, share, _ = soft_terms(other, neg_ref[...], positive)
        share_ref[here, :] = jnp.broadcast_to(share, (step, LANES))
        positive_ref[here, :] = jnp.broadcast_to(positive, (step, LANES))
        grad_ref[...] += inv_temp * dot(prob, other, ((0,), (0,)))

    grad = grad_ref[...]
    rows_sent = neg_ref[...].astype(F32)
    along = jnp.sum(grad * rows_sent, axis=1, keepdims=True)
    width = grad.shape[1]
    out_ref[:, :width] = (grad - along * rows_sent).astype(BF)
    lanes = lax.broadcasted_iota(jnp.int32, (grad.shape[0], LANES), 1)
    left = jnp.broadcast_to(along, lanes.shape)
    terms = jnp.zeros_like(left)
    for k in range(3):
        term = left.astype(BF).astype(F32)
        terms = jnp.where(lanes == k, term, terms)
        left = left - term
    out_ref[:, width:] = terms.astype(BF)


def backward(
    unit_ref, other_ref, neg_ref, share_ref, positive_ref, back_ref, pick_ref,
    normed_ref, scale_ref, w_ref, inv_ref, mixed_ref,
    loss_ref, scaled_ref, grad_ref, proj_ref
):
    rows, width = unit_ref.shape
    step = rows

    @pl.loop(0, 1)
    def _(c):
        here = rows_at(c, step)
        positive = positive_ref[here, :][:, :1]
        unit = unit_ref[here, :]
        prob, share, whole = soft_terms(unit, neg_ref[...], positive)
        loss = jnp.broadcast_to(jnp.log(whole) - positive, (step, LANES))
        loss_ref[:, here] = jnp.transpose(loss)[:1, :]
        other = other_ref[here, :].astype(F32)
        came = dot(pick_ref[:, here], back_ref[...], ((0,), (0,)))
        along = jnp.sum(came[:, width:], axis=1, keepdims=True)
        weight = inv_temp * share + inv_temp * share_ref[here, :][:, :1]
        grad = weight * other + inv_temp * dot(prob, neg_ref[...])
        grad = grad + (came[:, :width] + along * unit.astype(F32))
        normed = normed_ref[here, :]
        inner = jnp.sum(normed * grad, axis=1, keepdims=True)
        proj = ((grad - normed * inner) * wide(scale_ref[here, :], width)).astype(BF)
        proj_ref[here, :] = proj
        mixed = dot(proj, w_ref[...], ((1,), (1,)))
        scaled_ref[here, :] = (mixed * wide(inv_ref[here, :], width)).astype(BF)

    grad_ref[...] = dot(mixed_ref[...], proj_ref[...], ((0,), (0,)))


def mix_back(src_ref, tiles_ref, scaled_ref, own_ref, out_ref, total):
    blocks, tpb = src_ref.shape
    bs = tiles_ref.shape[1]
    rows = scaled_ref.shape[0]
    total[:rows, :] = scaled_ref[...].astype(F32)
    total[rows:, :] = jnp.zeros_like(total[rows:, :])

    @pl.loop(0, blocks, unroll=4)
    def _(b):
        spread = dot(tile_row(tiles_ref, b, tpb), scaled_ref[rows_at(b, bs), :], ((0,), (0,)))
        for t in range(tpb):
            total[rows_at(src_ref[b, t], bs), :] += spread[t * bs : (t + 1) * bs, :]

    own_ref[...] = total[:rows, :]
    out_ref[...] = total[rows:, :].astype(BF)


def finish(view_ref, own_ref, back_ref, send_ref, alive_ref, mixed_ref, second_ref, keep_ref, give_ref, grads):
    rows = own_ref.shape[0]
    step = rows

    @pl.loop(0, 1)
    def _(c):
        here = rows_at(c, step)
        grad = own_ref[here, :] + dot(send_ref[:, here], back_ref[...], ((0,), (0,)))
        grads[here, :] = jnp.where(alive_ref[here, :].astype(F32) > 0, grad, 0.0).astype(BF)

    first = dot(mixed_ref[...], grads[...], ((0,), (0,)))
    view = view_ref[0]

    @pl.when(view == 0)
    def _():
        keep_ref[...] = first
        give_ref[...] = second_ref[...]

    @pl.when(view != 0)
    def _():
        keep_ref[...] = second_ref[...]
        give_ref[...] = first


def per_device(
    features, feat_keep, w_first, w_second, adjacency, tile_src, halo_rows, halo_live, neg_pick
):
    rows, feat = features.shape
    hid = w_first.shape[1]
    bs = adjacency.shape[2]
    blocks, tpb = tile_src.shape[1:]
    parts = lax.axis_size("dom")
    slots = parts * halo_rows.shape[2]
    picks = parts * neg_pick.shape[2]
    mix_flops = 2 * blocks * tpb * bs * bs * hid
    dense_flops = 2 * rows * feat * hid

    halo_slots = jnp.swapaxes(halo_rows, 1, 2)[0]
    neg_slots = jnp.swapaxes(neg_pick, 1, 2)[0]
    view = lax.axis_index("view").reshape(1)
    outgoing, send, pick, masked, tiles, w_first, w_second, src = kernel_call(
        prepare,
        [shape(slots, feat, BF), shape(slots, rows, BF), shape(picks, rows, BF), features,
         adjacency[0], w_first, w_second, tile_src[0]],
        [halo_slots, halo_live, neg_slots, features, feat_keep, adjacency[0], w_first, w_second,
         tile_src[0]],
        [pltpu.SMEM(halo_slots.shape, jnp.int32), pltpu.SMEM(halo_live.shape, jnp.int32),
         pltpu.SMEM(neg_slots.shape, jnp.int32), pltpu.VMEM(features.shape, BF),
         pltpu.VMEM(feat_keep.shape, jnp.int32), pltpu.VMEM((max(slots, picks), LANES), jnp.int32),
         pltpu.SemaphoreType.DMA((9,))],
        space=pltpu.HBM,
    )
    incoming, send, pick, masked, tiles, w_first, w_second, src, view = to_others(
        outgoing, send, pick, masked, tiles, w_first, w_second, src, view
    )
    mixed_first, alive, hidden, inv_deg, outgoing = kernel_call(
        first_layer,
        [shape(rows, feat, BF), shape(rows, hid, BF), shape(rows, hid, BF), shape(rows, LANES, F32),
         shape(slots, hid, BF)],
        [src, masked, incoming, tiles, w_first, send],
        [pltpu.VMEM((rows + slots, feat), BF)],
        scalars=1, flops=mix_flops + dense_flops,
    )
    incoming, hidden, inv_deg, pick = to_others(outgoing, hidden, inv_deg, pick)
    mixed_second, normed, scale, unit, outgoing = kernel_call(
        second_layer,
        [shape(rows, hid, BF), shape(rows, hid, F32), shape(rows, LANES, F32), shape(rows, hid, BF),
         shape(picks, hid, BF)],
        [src, hidden, incoming, tiles, inv_deg, w_second, pick],
        [pltpu.VMEM((rows + slots, hid), BF)], scalars=1, flops=mix_flops + dense_flops,
    )
    other = exchange(unit, "view", 1)
    neg_other, unit = to_others(outgoing, unit)
    neg_own = exchange(neg_other, "view", 1)
    share, positive, grad_neg = kernel_call(
        contrast_other,
        [shape(rows, LANES, F32), shape(rows, LANES, F32), shape(picks, hid + LANES, BF)],
        [unit, other, neg_other], [pltpu.VMEM((picks, hid), F32)],
    )
    returned, neg_own, share, positive, unit, other = to_others(
        grad_neg, neg_own, share, positive, unit, other
    )
    loss, scaled, grad_second = kernel_call(
        backward,
        [shape(1, rows, F32), shape(rows, hid, BF), shape(hid, hid, F32)],
        [unit, other, neg_own, share, positive, returned, pick, normed, scale,
         w_second, inv_deg, mixed_second],
        [pltpu.VMEM((rows, hid), BF)], flops=2 * dense_flops,
    )
    own, outgoing = kernel_call(
        mix_back, [shape(rows, hid, F32), shape(slots, hid, BF)], [src, tiles, scaled],
        [pltpu.VMEM((rows + slots, hid), F32)], scalars=1, flops=mix_flops,
    )
    returned, own, grad_second, view, loss = to_others(outgoing, own, grad_second, view, loss)
    kept, given = kernel_call(
        finish, [shape(hid, hid, F32), shape(hid, hid, F32)],
        [view, own, returned, send, alive, mixed_first, grad_second],
        [pltpu.VMEM((rows, hid), BF)], scalars=1, flops=dense_flops,
    )
    pieces = (kept + exchange(given, "view", 1)).reshape(parts, -1, hid)
    summed = everyones_sum(pieces).reshape(-1, hid)
    swapped = exchange(summed, "view", 1)
    grad_first = jnp.where(view[0] == 0, summed, swapped)
    grad_second = jnp.where(view[0] == 0, swapped, summed)
    return (loss, grad_first, grad_second)


def solution(mesh):
    placed = (
        P("dom", None),
        P("view", None),
        P(),
        P(),
        P("view", "dom", None, None),
        P("view", "dom", None),
        P("dom", None, None),
        P("dom", None),
        P("dom", None, None),
    )
    return jax.shard_map(
        per_device,
        mesh=mesh,
        in_specs=placed,
        out_specs=(P("view", "dom"), P(), P()),
        check_vma=False,
    )
```

```python
import math

import jax
import jax.numpy as jnp
from jax import lax
from jax.experimental import pallas as pl
from jax.experimental.pallas import tpu as pltpu
from jax.sharding import PartitionSpec as P


inv_temp = 5.0
norm_eps = 1e-06
BF = jnp.bfloat16
F32 = jnp.float32
LANES = 128
SLACK = 6 * 2**20


def exchange(array, axis, distance):
    return lax.ppermute(array, axis, [(i, i ^ distance) for i in range(lax.axis_size(axis))])


def sum_slots():
    stages = []
    done = 1
    while done < lax.axis_size("dom"):
        ways = 4 if lax.axis_size("dom") // done % 4 == 0 else 2
        stages.append((ways, done))
        done *= ways
    turned = stages[::-1]
    if any(a[0] != b[0] for a, b in zip(stages, turned)):
        turned = stages
    return [(a[0], a[1], b[1]) for a, b in zip(stages, turned)]


def among(array, distances):
    parts = lax.axis_size("dom")
    pairs = [
        (view * parts + i, view * parts + (i ^ distances[min(view, 1)]))
        for view in range(lax.axis_size("view"))
        for i in range(parts)
    ]
    return lax.ppermute(array, ("view", "dom"), pairs)


def place_in(ways, stride, turned):
    part = lax.axis_index("dom")
    return jnp.where(lax.axis_index("view") == 0, part // stride, part // turned) % ways


def everyones_sum(pieces):
    slots = sum_slots()
    for ways, stride, turned in slots:
        mine = place_in(ways, stride, turned)
        split = pieces.reshape((ways, pieces.shape[0] // ways) + pieces.shape[1:])
        arrived = [
            among(lax.dynamic_index_in_dim(split, mine ^ d, 0, False), (d * stride, d * turned))
            for d in range(ways - 1, 0, -1)
        ]
        pieces = lax.dynamic_index_in_dim(split, mine, 0, False)
        for term in arrived:
            pieces = pieces + term
    for ways, stride, turned in slots[:0:-1]:
        mine = place_in(ways, stride, turned)
        held = [pieces] + [among(pieces, (d * stride, d * turned)) for d in range(1, ways)]
        ordered = []
        for j in range(ways):
            value = held[0]
            for d in range(1, ways):
                value = jnp.where(mine ^ j == d, held[d], value)
            ordered.append(value)
        pieces = jnp.concatenate(ordered, 0)
    ways, stride, turned = slots[0]
    held = [pieces] + [among(pieces, (d * stride, d * turned)) for d in range(1, ways)]
    part = lax.axis_index("dom")
    spots = jnp.stack([lax.axis_index("view"), part // stride % ways, part // turned % ways])
    return spots, held


def to_others(rows, *live):
    parts = lax.axis_size("dom")
    rows, live = lax.optimization_barrier((rows, live))
    split = rows.reshape(parts, rows.shape[0] // parts, rows.shape[1])
    moved = lax.all_to_all(split, "dom", split_axis=0, concat_axis=0, tiled=True)
    moved, live = lax.optimization_barrier((moved, live))
    return moved.reshape(rows.shape), *live


def kernel_call(body, outs, args, scratch=(), scalars=0, flops=0, space=pltpu.VMEM):
    moved = sum(a.size * a.dtype.itemsize for a in tuple(args) + tuple(outs))
    held = sum(math.prod(a.shape) * 4 for a in scratch)
    return pl.pallas_call(
        body,
        out_shape=tuple(jax.ShapeDtypeStruct(o.shape, o.dtype) for o in outs),
        in_specs=[pl.BlockSpec(memory_space=pltpu.SMEM)] * scalars
        + [pl.BlockSpec(memory_space=space)] * (len(args) - scalars),
        out_specs=tuple(pl.BlockSpec(memory_space=pltpu.VMEM) for _ in outs),
        scratch_shapes=list(scratch),
        cost_estimate=pl.CostEstimate(flops=flops, bytes_accessed=moved, transcendentals=0),
        compiler_params=pltpu.CompilerParams(vmem_limit_bytes=moved + held + SLACK),
        name=body.__name__ if hasattr(body, "__name__") else body.func.__name__,
    )(*(pltpu.with_memory_space_constraint(a, pltpu.HBM) if space == pltpu.HBM else a for a in args))


def shape(rows, cols, dtype):
    return jax.ShapeDtypeStruct((rows, cols), dtype)


def dot(a, b, dims=((1,), (0,))):
    return lax.dot_general(a, b, (dims, ((), ())), preferred_element_type=F32)


def pick_matrix(slots_ref, live_ref, place, width):
    cap, parts = slots_ref.shape

    @pl.loop(0, parts)
    def _(r):
        rows = lax.broadcasted_iota(jnp.int32, (cap, LANES), 0)
        slots = jnp.full((cap, LANES), -1, jnp.int32)
        for c in range(cap):
            slot = slots_ref[c, r]
            if live_ref is not None:
                slot = jnp.where(c < live_ref[0, r], slot, -1)
            slots = jnp.where(rows == c, slot, slots)
        place[rows_at(r, cap), :] = slots

    slots = place[...]
    lanes = lax.broadcasted_iota(jnp.int32, slots.shape, 1)
    columns = [
        jnp.where(slots == lanes + first, 1.0, 0.0).astype(BF) for first in range(0, width, LANES)
    ]
    return jnp.concatenate(columns, axis=1)


def wide(column, width):
    return jnp.concatenate([column] * (width // LANES), axis=1)


def rows_at(index, size):
    return pl.ds(pl.multiple_of(index * size, size), size)


def prepare(
    slots_hbm, live_hbm, picks_hbm, feat_hbm, keep_hbm, tiles_hbm, first_hbm, second_hbm, src_hbm,
    out_ref, send_ref, pick_ref, masked_ref, tiles_ref, first_ref, second_ref, src_ref,
    slots, live, picks, feat, keep, place, sems
):
    pairs = [
        (slots_hbm, slots), (live_hbm, live), (feat_hbm, feat), (keep_hbm, keep),
        (picks_hbm, picks), (src_hbm, src_ref), (tiles_hbm, tiles_ref), (first_hbm, first_ref),
        (second_hbm, second_ref),
    ]
    copies = [pltpu.make_async_copy(a, b, sems.at[k]) for k, (a, b) in enumerate(pairs)]
    for copy in copies:
        copy.start()
    copies[0].wait()
    copies[1].wait()
    send_ref[...] = pick_matrix(slots, live, place, feat.shape[0])
    copies[2].wait()
    copies[3].wait()
    masked = feat[...] * keep[...].astype(F32).astype(BF)
    masked_ref[...] = masked
    out_ref[...] = dot(send_ref[...], masked).astype(BF)
    copies[4].wait()
    pick_ref[...] = pick_matrix(picks, None, place, feat.shape[0])
    for copy in copies[5:]:
        copy.wait()


def tile_row(tiles_ref, b, tpb):
    return jnp.concatenate([tiles_ref[b * tpb + t] for t in range(tpb)], axis=1)


def mixed_sum(src_ref, tiles, ext, b, bs):
    picked = [ext[rows_at(src_ref[b, t], bs), :] for t in range(src_ref.shape[1])]
    return dot(tiles, jnp.concatenate(picked, axis=0)) + ext[rows_at(b, bs), :].astype(F32)


def first_layer(
    src_ref, masked_ref, halo_ref, tiles_ref, w_ref, send_ref,
    mixed_ref, alive_ref, hidden_ref, inv_ref, out_ref, ext
):
    blocks, tpb = src_ref.shape
    bs = tiles_ref.shape[1]
    rows, width = masked_ref.shape
    ext[:rows, :] = masked_ref[...]
    ext[rows:, :] = halo_ref[...]

    @pl.loop(0, blocks, unroll=True)
    def _(b):
        here = rows_at(b, bs)
        tiles = tile_row(tiles_ref, b, tpb)
        inv = 1.0 / (1.0 + dot(tiles, jnp.ones((tpb * bs, LANES), BF)))
        inv_ref[here, :] = inv
        mixed_ref[here, :] = (mixed_sum(src_ref, tiles, ext, b, bs) * wide(inv, width)).astype(BF)

    step = rows

    @pl.loop(0, 1)
    def _(c):
        here = rows_at(c, step)
        pre = dot(mixed_ref[here, :], w_ref[...])
        alive_ref[here, :] = jnp.where(pre > 0, 1.0, 0.0).astype(BF)
        hidden_ref[here, :] = jnp.maximum(pre, 0.0).astype(BF)

    out_ref[...] = dot(send_ref[...], hidden_ref[...]).astype(BF)


def second_layer(
    src_ref, hidden_ref, halo_ref, tiles_ref, inv_ref, w_ref, pick_ref,
    mixed_ref, normed_ref, scale_ref, unit_ref, out_ref, ext
):
    blocks, tpb = src_ref.shape
    bs = tiles_ref.shape[1]
    rows, width = hidden_ref.shape
    ext[:rows, :] = hidden_ref[...]
    ext[rows:, :] = halo_ref[...]

    @pl.loop(0, blocks, unroll=True)
    def _(b):
        here = rows_at(b, bs)
        total = mixed_sum(src_ref, tile_row(tiles_ref, b, tpb), ext, b, bs)
        mixed_ref[here, :] = (total * wide(inv_ref[here, :], width)).astype(BF)

    step = rows

    @pl.loop(0, 1)
    def _(c):
        here = rows_at(c, step)
        projected = dot(mixed_ref[here, :], w_ref[...])
        scale = lax.rsqrt(jnp.sum(projected * projected, axis=1, keepdims=True) + norm_eps)
        normed = projected * scale
        normed_ref[here, :] = normed
        scale_ref[here, :] = jnp.broadcast_to(scale, (step, LANES))
        unit_ref[here, :] = normed.astype(BF)

    out_ref[...] = dot(pick_ref[...], unit_ref[...]).astype(BF)


def soft_terms(anchor, negatives, positive):
    expo = jnp.exp(inv_temp * dot(anchor, negatives, ((1,), (1,))))
    top = jnp.exp(positive)
    total = top + jnp.sum(expo, axis=1, keepdims=True)
    return (expo / total).astype(BF), top / total - 1.0, total


def contrast_other(unit_ref, other_ref, neg_ref, share_ref, positive_ref, out_ref, grad_ref):
    rows = unit_ref.shape[0]
    step = rows
    grad_ref[...] = jnp.zeros_like(grad_ref)

    @pl.loop(0, 1)
    def _(c):
        here = rows_at(c, step)
        other = other_ref[here, :]
        product = unit_ref[here, :].astype(F32) * other.astype(F32)
        positive = inv_temp * jnp.sum(product, axis=1, keepdims=True)
        prob, share, _ = soft_terms(other, neg_ref[...], positive)
        share_ref[here, :] = jnp.broadcast_to(share, (step, LANES))
        positive_ref[here, :] = jnp.broadcast_to(positive, (step, LANES))
        grad_ref[...] += inv_temp * dot(prob, other, ((0,), (0,)))

    grad = grad_ref[...]
    rows_sent = neg_ref[...].astype(F32)
    along = jnp.sum(grad * rows_sent, axis=1, keepdims=True)
    width = grad.shape[1]
    out_ref[:, :width] = (grad - along * rows_sent).astype(BF)
    lanes = lax.broadcasted_iota(jnp.int32, (grad.shape[0], LANES), 1)
    left = jnp.broadcast_to(along, lanes.shape)
    terms = jnp.zeros_like(left)
    for k in range(3):
        term = left.astype(BF).astype(F32)
        terms = jnp.where(lanes == k, term, terms)
        left = left - term
    out_ref[:, width:] = terms.astype(BF)


def backward(
    unit_ref, other_ref, neg_ref, share_ref, positive_ref, back_ref, pick_ref,
    normed_ref, scale_ref, w_ref, inv_ref, mixed_ref,
    loss_ref, scaled_ref, grad_ref, proj_ref
):
    rows, width = unit_ref.shape
    step = rows

    @pl.loop(0, 1)
    def _(c):
        here = rows_at(c, step)
        positive = positive_ref[here, :][:, :1]
        unit = unit_ref[here, :]
        prob, share, whole = soft_terms(unit, neg_ref[...], positive)
        loss = jnp.broadcast_to(jnp.log(whole) - positive, (step, LANES))
        loss_ref[:, here] = jnp.transpose(loss)[:1, :]
        other = other_ref[here, :].astype(F32)
        came = dot(pick_ref[:, here], back_ref[...], ((0,), (0,)))
        along = jnp.sum(came[:, width:], axis=1, keepdims=True)
        weight = inv_temp * share + inv_temp * share_ref[here, :][:, :1]
        grad = weight * other + inv_temp * dot(prob, neg_ref[...])
        grad = grad + (came[:, :width] + along * unit.astype(F32))
        normed = normed_ref[here, :]
        inner = jnp.sum(normed * grad, axis=1, keepdims=True)
        proj = ((grad - normed * inner) * wide(scale_ref[here, :], width)).astype(BF)
        proj_ref[here, :] = proj
        mixed = dot(proj, w_ref[...], ((1,), (1,)))
        scaled_ref[here, :] = (mixed * wide(inv_ref[here, :], width)).astype(BF)

    grad_ref[...] = dot(mixed_ref[...], proj_ref[...], ((0,), (0,)))


def mix_back(src_ref, tiles_ref, scaled_ref, own_ref, out_ref, total):
    blocks, tpb = src_ref.shape
    bs = tiles_ref.shape[1]
    rows = scaled_ref.shape[0]
    total[:rows, :] = scaled_ref[...].astype(F32)
    total[rows:, :] = jnp.zeros_like(total[rows:, :])

    @pl.loop(0, blocks, unroll=4)
    def _(b):
        spread = dot(tile_row(tiles_ref, b, tpb), scaled_ref[rows_at(b, bs), :], ((0,), (0,)))
        for t in range(tpb):
            total[rows_at(src_ref[b, t], bs), :] += spread[t * bs : (t + 1) * bs, :]

    own_ref[...] = total[:rows, :]
    out_ref[...] = total[rows:, :].astype(BF)


def finish(view_ref, own_ref, back_ref, send_ref, alive_ref, mixed_ref, second_ref, keep_ref, give_ref, grads):
    rows = own_ref.shape[0]
    step = rows

    @pl.loop(0, 1)
    def _(c):
        here = rows_at(c, step)
        grad = own_ref[here, :] + dot(send_ref[:, here], back_ref[...], ((0,), (0,)))
        grads[here, :] = jnp.where(alive_ref[here, :].astype(F32) > 0, grad, 0.0).astype(BF)

    first = dot(mixed_ref[...], grads[...], ((0,), (0,)))
    view = view_ref[0]

    @pl.when(view == 0)
    def _():
        keep_ref[...] = first
        give_ref[...] = second_ref[...]

    @pl.when(view != 0)
    def _():
        keep_ref[...] = second_ref[...]
        give_ref[...] = first


def assemble(spots_ref, *refs):
    ways = (len(refs) - 2) // 2
    held, others, first_ref, second_ref = refs[:ways], refs[ways:-2], refs[-2], refs[-1]
    size = held[0].shape[0]

    def fill(firsts, seconds):
        for d in range(ways):
            first_ref[rows_at(spots_ref[1] ^ d, size), :] = firsts[d][...]
            second_ref[rows_at(spots_ref[2] ^ d, size), :] = seconds[d][...]

    @pl.when(spots_ref[0] == 0)
    def _():
        fill(held, others)

    @pl.when(spots_ref[0] != 0)
    def _():
        fill(others, held)


def per_device(
    features, feat_keep, w_first, w_second, adjacency, tile_src, halo_rows, halo_live, neg_pick
):
    rows, feat = features.shape
    hid = w_first.shape[1]
    bs = adjacency.shape[2]
    blocks, tpb = tile_src.shape[1:]
    parts = lax.axis_size("dom")
    slots = parts * halo_rows.shape[2]
    picks = parts * neg_pick.shape[2]
    mix_flops = 2 * blocks * tpb * bs * bs * hid
    dense_flops = 2 * rows * feat * hid

    halo_slots = jnp.swapaxes(halo_rows, 1, 2)[0]
    neg_slots = jnp.swapaxes(neg_pick, 1, 2)[0]
    view = lax.axis_index("view").reshape(1)
    outgoing, send, pick, masked, tiles, w_first, w_second, src = kernel_call(
        prepare,
        [shape(slots, feat, BF), shape(slots, rows, BF), shape(picks, rows, BF), features,
         adjacency[0], w_first, w_second, tile_src[0]],
        [halo_slots, halo_live, neg_slots, features, feat_keep, adjacency[0], w_first, w_second,
         tile_src[0]],
        [pltpu.SMEM(halo_slots.shape, jnp.int32), pltpu.SMEM(halo_live.shape, jnp.int32),
         pltpu.SMEM(neg_slots.shape, jnp.int32), pltpu.VMEM(features.shape, BF),
         pltpu.VMEM(feat_keep.shape, jnp.int32), pltpu.VMEM((max(slots, picks), LANES), jnp.int32),
         pltpu.SemaphoreType.DMA((9,))],
        space=pltpu.HBM,
    )
    incoming, send, pick, masked, tiles, w_first, w_second, src, view = to_others(
        outgoing, send, pick, masked, tiles, w_first, w_second, src, view
    )
    mixed_first, alive, hidden, inv_deg, outgoing = kernel_call(
        first_layer,
        [shape(rows, feat, BF), shape(rows, hid, BF), shape(rows, hid, BF), shape(rows, LANES, F32),
         shape(slots, hid, BF)],
        [src, masked, incoming, tiles, w_first, send],
        [pltpu.VMEM((rows + slots, feat), BF)],
        scalars=1, flops=mix_flops + dense_flops,
    )
    incoming, hidden, inv_deg, pick = to_others(outgoing, hidden, inv_deg, pick)
    mixed_second, normed, scale, unit, outgoing = kernel_call(
        second_layer,
        [shape(rows, hid, BF), shape(rows, hid, F32), shape(rows, LANES, F32), shape(rows, hid, BF),
         shape(picks, hid, BF)],
        [src, hidden, incoming, tiles, inv_deg, w_second, pick],
        [pltpu.VMEM((rows + slots, hid), BF)], scalars=1, flops=mix_flops + dense_flops,
    )
    other = exchange(unit, "view", 1)
    neg_other, unit = to_others(outgoing, unit)
    neg_own = exchange(neg_other, "view", 1)
    share, positive, grad_neg = kernel_call(
        contrast_other,
        [shape(rows, LANES, F32), shape(rows, LANES, F32), shape(picks, hid + LANES, BF)],
        [unit, other, neg_other], [pltpu.VMEM((picks, hid), F32)],
    )
    returned, neg_own, share, positive, unit, other = to_others(
        grad_neg, neg_own, share, positive, unit, other
    )
    loss, scaled, grad_second = kernel_call(
        backward,
        [shape(1, rows, F32), shape(rows, hid, BF), shape(hid, hid, F32)],
        [unit, other, neg_own, share, positive, returned, pick, normed, scale,
         w_second, inv_deg, mixed_second],
        [pltpu.VMEM((rows, hid), BF)], flops=2 * dense_flops,
    )
    own, outgoing = kernel_call(
        mix_back, [shape(rows, hid, F32), shape(slots, hid, BF)], [src, tiles, scaled],
        [pltpu.VMEM((rows + slots, hid), F32)], scalars=1, flops=mix_flops,
    )
    returned, own, grad_second, view, loss = to_others(outgoing, own, grad_second, view, loss)
    kept, given = kernel_call(
        finish, [shape(hid, hid, F32), shape(hid, hid, F32)],
        [view, own, returned, send, alive, mixed_first, grad_second],
        [pltpu.VMEM((rows, hid), BF)], scalars=1, flops=dense_flops,
    )
    pieces = (kept + exchange(given, "view", 1)).reshape(parts, -1, hid)
    spots, held = everyones_sum(pieces)
    held = [piece.reshape(-1, hid) for piece in held]
    others = [exchange(piece, "view", 1) for piece in held]
    grad_first, grad_second = kernel_call(
        assemble, [shape(feat, hid, F32), shape(hid, hid, F32)], [spots, *held, *others], scalars=1
    )
    return (loss, grad_first, grad_second)


def solution(mesh):
    placed = (
        P("dom", None),
        P("view", None),
        P(),
        P(),
        P("view", "dom", None, None),
        P("view", "dom", None),
        P("dom", None, None),
        P("dom", None),
        P("dom", None, None),
    )
    return jax.shard_map(
        per_device,
        mesh=mesh,
        in_specs=placed,
        out_specs=(P("view", "dom"), P(), P()),
        check_vma=False,
    )
```

```python
import math

import jax
import jax.numpy as jnp
from jax import lax
from jax.experimental import pallas as pl
from jax.experimental.pallas import tpu as pltpu
from jax.sharding import PartitionSpec as P


inv_temp = 5.0
norm_eps = 1e-06
BF = jnp.bfloat16
F32 = jnp.float32
LANES = 128
SLACK = 6 * 2**20


def exchange(array, axis, distance):
    return lax.ppermute(array, axis, [(i, i ^ distance) for i in range(lax.axis_size(axis))])


def sum_slots():
    stages = []
    done = 1
    while done < lax.axis_size("dom"):
        ways = 4 if lax.axis_size("dom") // done % 4 == 0 else 2
        stages.append((ways, done))
        done *= ways
    turned = stages[::-1]
    if any(a[0] != b[0] for a, b in zip(stages, turned)):
        turned = stages
    return [(a[0], a[1], b[1]) for a, b in zip(stages, turned)]


def among(array, distances):
    parts = lax.axis_size("dom")
    pairs = [
        (view * parts + i, view * parts + (i ^ distances[min(view, 1)]))
        for view in range(lax.axis_size("view"))
        for i in range(parts)
    ]
    return lax.ppermute(array, ("view", "dom"), pairs)


def place_in(ways, stride, turned):
    part = lax.axis_index("dom")
    return jnp.where(lax.axis_index("view") == 0, part // stride, part // turned) % ways


def everyones_sum(pieces):
    slots = sum_slots()
    for ways, stride, turned in slots:
        mine = place_in(ways, stride, turned)
        split = pieces.reshape((ways, pieces.shape[0] // ways) + pieces.shape[1:])
        arrived = [
            among(lax.dynamic_index_in_dim(split, mine ^ d, 0, False), (d * stride, d * turned))
            for d in range(ways - 1, 0, -1)
        ]
        pieces = lax.dynamic_index_in_dim(split, mine, 0, False)
        for term in arrived:
            pieces = pieces + term
    for ways, stride, turned in slots[:0:-1]:
        mine = place_in(ways, stride, turned)
        held = [pieces] + [among(pieces, (d * stride, d * turned)) for d in range(1, ways)]
        ordered = []
        for j in range(ways):
            value = held[0]
            for d in range(1, ways):
                value = jnp.where(mine ^ j == d, held[d], value)
            ordered.append(value)
        pieces = jnp.concatenate(ordered, 0)
    ways, stride, turned = slots[0]
    held = [pieces] + [among(pieces, (d * stride, d * turned)) for d in range(1, ways)]
    part = lax.axis_index("dom")
    spots = jnp.stack([lax.axis_index("view"), part // stride % ways, part // turned % ways])
    return spots, held


def to_others(rows, *live):
    parts = lax.axis_size("dom")
    rows, live = lax.optimization_barrier((rows, live))
    split = rows.reshape(parts, rows.shape[0] // parts, rows.shape[1])
    moved = lax.all_to_all(split, "dom", split_axis=0, concat_axis=0, tiled=True)
    moved, live = lax.optimization_barrier((moved, live))
    return moved.reshape(rows.shape), *live


def kernel_call(body, outs, args, scratch=(), scalars=0, flops=0, space=pltpu.VMEM):
    moved = sum(a.size * a.dtype.itemsize for a in tuple(args) + tuple(outs))
    held = sum(math.prod(a.shape) * 4 for a in scratch)
    return pl.pallas_call(
        body,
        out_shape=tuple(jax.ShapeDtypeStruct(o.shape, o.dtype) for o in outs),
        in_specs=[pl.BlockSpec(memory_space=pltpu.SMEM)] * scalars
        + [pl.BlockSpec(memory_space=space)] * (len(args) - scalars),
        out_specs=tuple(pl.BlockSpec(memory_space=pltpu.VMEM) for _ in outs),
        scratch_shapes=list(scratch),
        cost_estimate=pl.CostEstimate(flops=flops, bytes_accessed=moved, transcendentals=0),
        compiler_params=pltpu.CompilerParams(vmem_limit_bytes=moved + held + SLACK),
        name=body.__name__ if hasattr(body, "__name__") else body.func.__name__,
    )(*(pltpu.with_memory_space_constraint(a, pltpu.HBM) if space == pltpu.HBM else a for a in args))


def shape(rows, cols, dtype):
    return jax.ShapeDtypeStruct((rows, cols), dtype)


def dot(a, b, dims=((1,), (0,))):
    return lax.dot_general(a, b, (dims, ((), ())), preferred_element_type=F32)


def pick_matrix(slots_ref, live_ref, place, width):
    cap, parts = slots_ref.shape

    @pl.loop(0, parts)
    def _(r):
        rows = lax.broadcasted_iota(jnp.int32, (cap, LANES), 0)
        slots = jnp.full((cap, LANES), -1, jnp.int32)
        for c in range(cap):
            slot = slots_ref[c, r]
            if live_ref is not None:
                slot = jnp.where(c < live_ref[0, r], slot, -1)
            slots = jnp.where(rows == c, slot, slots)
        place[rows_at(r, cap), :] = slots

    slots = place[...]
    lanes = lax.broadcasted_iota(jnp.int32, slots.shape, 1)
    columns = [
        jnp.where(slots == lanes + first, 1.0, 0.0).astype(BF) for first in range(0, width, LANES)
    ]
    return jnp.concatenate(columns, axis=1)


def wide(column, width):
    return jnp.concatenate([column] * (width // LANES), axis=1)


def rows_at(index, size):
    return pl.ds(pl.multiple_of(index * size, size), size)


def prepare(
    slots_hbm, live_hbm, picks_hbm, feat_hbm, keep_hbm, tiles_hbm, first_hbm, src_hbm,
    out_ref, send_ref, pick_ref, masked_ref, tiles_ref, first_ref, src_ref,
    slots, live, picks, feat, keep, place, sems
):
    pairs = [
        (slots_hbm, slots), (live_hbm, live), (feat_hbm, feat), (keep_hbm, keep),
        (picks_hbm, picks), (src_hbm, src_ref), (tiles_hbm, tiles_ref), (first_hbm, first_ref),
    ]
    copies = [pltpu.make_async_copy(a, b, sems.at[k]) for k, (a, b) in enumerate(pairs)]
    for copy in copies:
        copy.start()
    copies[0].wait()
    copies[1].wait()
    send_ref[...] = pick_matrix(slots, live, place, feat.shape[0])
    copies[2].wait()
    copies[3].wait()
    masked = feat[...] * keep[...].astype(F32).astype(BF)
    masked_ref[...] = masked
    out_ref[...] = dot(send_ref[...], masked).astype(BF)
    copies[4].wait()
    pick_ref[...] = pick_matrix(picks, None, place, feat.shape[0])
    for copy in copies[5:]:
        copy.wait()


def tile_row(tiles_ref, b, tpb):
    return jnp.concatenate([tiles_ref[b * tpb + t] for t in range(tpb)], axis=1)


def mixed_sum(src_ref, tiles, ext, b, bs):
    picked = [ext[rows_at(src_ref[b, t], bs), :] for t in range(src_ref.shape[1])]
    return dot(tiles, jnp.concatenate(picked, axis=0)) + ext[rows_at(b, bs), :].astype(F32)


def first_layer(
    src_ref, masked_ref, halo_ref, tiles_ref, w_ref, send_ref,
    mixed_ref, alive_ref, hidden_ref, inv_ref, out_ref, ext
):
    blocks, tpb = src_ref.shape
    bs = tiles_ref.shape[1]
    rows, width = masked_ref.shape
    ext[:rows, :] = masked_ref[...]
    ext[rows:, :] = halo_ref[...]

    @pl.loop(0, blocks, unroll=True)
    def _(b):
        here = rows_at(b, bs)
        tiles = tile_row(tiles_ref, b, tpb)
        inv = 1.0 / (1.0 + dot(tiles, jnp.ones((tpb * bs, LANES), BF)))
        inv_ref[here, :] = inv
        mixed_ref[here, :] = (mixed_sum(src_ref, tiles, ext, b, bs) * wide(inv, width)).astype(BF)

    step = rows

    @pl.loop(0, 1)
    def _(c):
        here = rows_at(c, step)
        pre = dot(mixed_ref[here, :], w_ref[...])
        alive_ref[here, :] = jnp.where(pre > 0, 1.0, 0.0).astype(BF)
        hidden_ref[here, :] = jnp.maximum(pre, 0.0).astype(BF)

    out_ref[...] = dot(send_ref[...], hidden_ref[...]).astype(BF)


def second_layer(
    src_ref, hidden_ref, halo_ref, tiles_ref, inv_ref, w_ref, pick_ref,
    mixed_ref, normed_ref, scale_ref, unit_ref, out_ref, ext
):
    blocks, tpb = src_ref.shape
    bs = tiles_ref.shape[1]
    rows, width = hidden_ref.shape
    ext[:rows, :] = hidden_ref[...]
    ext[rows:, :] = halo_ref[...]

    @pl.loop(0, blocks, unroll=True)
    def _(b):
        here = rows_at(b, bs)
        total = mixed_sum(src_ref, tile_row(tiles_ref, b, tpb), ext, b, bs)
        mixed_ref[here, :] = (total * wide(inv_ref[here, :], width)).astype(BF)

    step = rows

    @pl.loop(0, 1)
    def _(c):
        here = rows_at(c, step)
        projected = dot(mixed_ref[here, :], w_ref[...])
        scale = lax.rsqrt(jnp.sum(projected * projected, axis=1, keepdims=True) + norm_eps)
        normed = projected * scale
        normed_ref[here, :] = normed
        scale_ref[here, :] = jnp.broadcast_to(scale, (step, LANES))
        unit_ref[here, :] = normed.astype(BF)

    out_ref[...] = dot(pick_ref[...], unit_ref[...]).astype(BF)


def soft_terms(anchor, negatives, positive):
    expo = jnp.exp(inv_temp * dot(anchor, negatives, ((1,), (1,))))
    top = jnp.exp(positive)
    total = top + jnp.sum(expo, axis=1, keepdims=True)
    return (expo / total).astype(BF), top / total - 1.0, total


def contrast_other(unit_ref, other_ref, neg_ref, share_ref, positive_ref, out_ref, grad_ref):
    rows = unit_ref.shape[0]
    step = rows
    grad_ref[...] = jnp.zeros_like(grad_ref)

    @pl.loop(0, 1)
    def _(c):
        here = rows_at(c, step)
        other = other_ref[here, :]
        product = unit_ref[here, :].astype(F32) * other.astype(F32)
        positive = inv_temp * jnp.sum(product, axis=1, keepdims=True)
        prob, share, _ = soft_terms(other, neg_ref[...], positive)
        share_ref[here, :] = jnp.broadcast_to(share, (step, LANES))
        positive_ref[here, :] = jnp.broadcast_to(positive, (step, LANES))
        grad_ref[...] += inv_temp * dot(prob, other, ((0,), (0,)))

    grad = grad_ref[...]
    rows_sent = neg_ref[...].astype(F32)
    along = jnp.sum(grad * rows_sent, axis=1, keepdims=True)
    width = grad.shape[1]
    out_ref[:, :width] = (grad - along * rows_sent).astype(BF)
    lanes = lax.broadcasted_iota(jnp.int32, (grad.shape[0], LANES), 1)
    left = jnp.broadcast_to(along, lanes.shape)
    terms = jnp.zeros_like(left)
    for k in range(3):
        term = left.astype(BF).astype(F32)
        terms = jnp.where(lanes == k, term, terms)
        left = left - term
    out_ref[:, width:] = terms.astype(BF)


def backward(
    unit_ref, other_ref, neg_ref, share_ref, positive_ref, back_ref, pick_ref,
    normed_ref, scale_ref, w_ref, inv_ref, mixed_ref,
    loss_ref, scaled_ref, grad_ref, proj_ref
):
    rows, width = unit_ref.shape
    step = rows

    @pl.loop(0, 1)
    def _(c):
        here = rows_at(c, step)
        positive = positive_ref[here, :][:, :1]
        unit = unit_ref[here, :]
        prob, share, whole = soft_terms(unit, neg_ref[...], positive)
        loss = jnp.broadcast_to(jnp.log(whole) - positive, (step, LANES))
        loss_ref[:, here] = jnp.transpose(loss)[:1, :]
        other = other_ref[here, :].astype(F32)
        came = dot(pick_ref[:, here], back_ref[...], ((0,), (0,)))
        along = jnp.sum(came[:, width:], axis=1, keepdims=True)
        weight = inv_temp * share + inv_temp * share_ref[here, :][:, :1]
        grad = weight * other + inv_temp * dot(prob, neg_ref[...])
        grad = grad + (came[:, :width] + along * unit.astype(F32))
        normed = normed_ref[here, :]
        inner = jnp.sum(normed * grad, axis=1, keepdims=True)
        proj = ((grad - normed * inner) * wide(scale_ref[here, :], width)).astype(BF)
        proj_ref[here, :] = proj
        mixed = dot(proj, w_ref[...], ((1,), (1,)))
        scaled_ref[here, :] = (mixed * wide(inv_ref[here, :], width)).astype(BF)

    grad_ref[...] = dot(mixed_ref[...], proj_ref[...], ((0,), (0,)))


def mix_back(src_ref, tiles_ref, scaled_ref, own_ref, out_ref, total):
    blocks, tpb = src_ref.shape
    bs = tiles_ref.shape[1]
    rows = scaled_ref.shape[0]
    total[:rows, :] = scaled_ref[...].astype(F32)
    total[rows:, :] = jnp.zeros_like(total[rows:, :])

    @pl.loop(0, blocks, unroll=4)
    def _(b):
        spread = dot(tile_row(tiles_ref, b, tpb), scaled_ref[rows_at(b, bs), :], ((0,), (0,)))
        for t in range(tpb):
            total[rows_at(src_ref[b, t], bs), :] += spread[t * bs : (t + 1) * bs, :]

    own_ref[...] = total[:rows, :]
    out_ref[...] = total[rows:, :].astype(BF)


def finish(view_ref, own_ref, back_ref, send_ref, alive_ref, mixed_ref, second_ref, keep_ref, give_ref, grads):
    rows = own_ref.shape[0]
    step = rows

    @pl.loop(0, 1)
    def _(c):
        here = rows_at(c, step)
        grad = own_ref[here, :] + dot(send_ref[:, here], back_ref[...], ((0,), (0,)))
        grads[here, :] = jnp.where(alive_ref[here, :].astype(F32) > 0, grad, 0.0).astype(BF)

    first = dot(mixed_ref[...], grads[...], ((0,), (0,)))
    view = view_ref[0]

    @pl.when(view == 0)
    def _():
        keep_ref[...] = first
        give_ref[...] = second_ref[...]

    @pl.when(view != 0)
    def _():
        keep_ref[...] = second_ref[...]
        give_ref[...] = first


def assemble(spots_ref, *refs):
    ways = (len(refs) - 2) // 2
    held, others, first_ref, second_ref = refs[:ways], refs[ways:-2], refs[-2], refs[-1]
    size = held[0].shape[0]

    def fill(firsts, seconds):
        for d in range(ways):
            first_ref[rows_at(spots_ref[1] ^ d, size), :] = firsts[d][...]
            second_ref[rows_at(spots_ref[2] ^ d, size), :] = seconds[d][...]

    @pl.when(spots_ref[0] == 0)
    def _():
        fill(held, others)

    @pl.when(spots_ref[0] != 0)
    def _():
        fill(others, held)


def per_device(
    features, feat_keep, w_first, w_second, adjacency, tile_src, halo_rows, halo_live, neg_pick
):
    rows, feat = features.shape
    hid = w_first.shape[1]
    bs = adjacency.shape[2]
    blocks, tpb = tile_src.shape[1:]
    parts = lax.axis_size("dom")
    slots = parts * halo_rows.shape[2]
    picks = parts * neg_pick.shape[2]
    mix_flops = 2 * blocks * tpb * bs * bs * hid
    dense_flops = 2 * rows * feat * hid

    halo_slots = jnp.swapaxes(halo_rows, 1, 2)[0]
    neg_slots = jnp.swapaxes(neg_pick, 1, 2)[0]
    view = lax.axis_index("view").reshape(1)
    outgoing, send, pick, masked, tiles, w_first, src = kernel_call(
        prepare,
        [shape(slots, feat, BF), shape(slots, rows, BF), shape(picks, rows, BF), features,
         adjacency[0], w_first, tile_src[0]],
        [halo_slots, halo_live, neg_slots, features, feat_keep, adjacency[0], w_first,
         tile_src[0]],
        [pltpu.SMEM(halo_slots.shape, jnp.int32), pltpu.SMEM(halo_live.shape, jnp.int32),
         pltpu.SMEM(neg_slots.shape, jnp.int32), pltpu.VMEM(features.shape, BF),
         pltpu.VMEM(feat_keep.shape, jnp.int32), pltpu.VMEM((max(slots, picks), LANES), jnp.int32),
         pltpu.SemaphoreType.DMA((8,))],
        space=pltpu.HBM,
    )
    incoming, send, pick, masked, tiles, w_first, src, view = to_others(
        outgoing, send, pick, masked, tiles, w_first, src, view
    )
    mixed_first, alive, hidden, inv_deg, outgoing = kernel_call(
        first_layer,
        [shape(rows, feat, BF), shape(rows, hid, BF), shape(rows, hid, BF), shape(rows, LANES, F32),
         shape(slots, hid, BF)],
        [src, masked, incoming, tiles, w_first, send],
        [pltpu.VMEM((rows + slots, feat), BF)],
        scalars=1, flops=mix_flops + dense_flops,
    )
    incoming, hidden, inv_deg, pick = to_others(outgoing, hidden, inv_deg, pick)
    mixed_second, normed, scale, unit, outgoing = kernel_call(
        second_layer,
        [shape(rows, hid, BF), shape(rows, hid, F32), shape(rows, LANES, F32), shape(rows, hid, BF),
         shape(picks, hid, BF)],
        [src, hidden, incoming, tiles, inv_deg, w_second, pick],
        [pltpu.VMEM((rows + slots, hid), BF)], scalars=1, flops=mix_flops + dense_flops,
    )
    other = exchange(unit, "view", 1)
    neg_other, unit = to_others(outgoing, unit)
    neg_own = exchange(neg_other, "view", 1)
    share, positive, grad_neg = kernel_call(
        contrast_other,
        [shape(rows, LANES, F32), shape(rows, LANES, F32), shape(picks, hid + LANES, BF)],
        [unit, other, neg_other], [pltpu.VMEM((picks, hid), F32)],
    )
    returned, neg_own, share, positive, unit, other = to_others(
        grad_neg, neg_own, share, positive, unit, other
    )
    loss, scaled, grad_second = kernel_call(
        backward,
        [shape(1, rows, F32), shape(rows, hid, BF), shape(hid, hid, F32)],
        [unit, other, neg_own, share, positive, returned, pick, normed, scale,
         w_second, inv_deg, mixed_second],
        [pltpu.VMEM((rows, hid), BF)], flops=2 * dense_flops,
    )
    own, outgoing = kernel_call(
        mix_back, [shape(rows, hid, F32), shape(slots, hid, BF)], [src, tiles, scaled],
        [pltpu.VMEM((rows + slots, hid), F32)], scalars=1, flops=mix_flops,
    )
    returned, own, grad_second, view, loss = to_others(outgoing, own, grad_second, view, loss)
    kept, given = kernel_call(
        finish, [shape(hid, hid, F32), shape(hid, hid, F32)],
        [view, own, returned, send, alive, mixed_first, grad_second],
        [pltpu.VMEM((rows, hid), BF)], scalars=1, flops=dense_flops,
    )
    pieces = (kept + exchange(given, "view", 1)).reshape(parts, -1, hid)
    spots, held = everyones_sum(pieces)
    held = [piece.reshape(-1, hid) for piece in held]
    others = [exchange(piece, "view", 1) for piece in held]
    grad_first, grad_second = kernel_call(
        assemble, [shape(feat, hid, F32), shape(hid, hid, F32)], [spots, *held, *others], scalars=1
    )
    return (loss, grad_first, grad_second)


def solution(mesh):
    placed = (
        P("dom", None),
        P("view", None),
        P(),
        P(),
        P("view", "dom", None, None),
        P("view", "dom", None),
        P("dom", None, None),
        P("dom", None),
        P("dom", None, None),
    )
    return jax.shard_map(
        per_device,
        mesh=mesh,
        in_specs=placed,
        out_specs=(P("view", "dom"), P(), P()),
        check_vma=False,
    )
```
